256 devices in a mesh: blk: 32 (over z, y), aux: 8 (over x, core).
Axes of the slice: x: 4, y: 4, z: 8, core: 2. Of those that a mesh axis runs over, the one named last changes fastest.
Arguments:
- adjoint: bfloat16 [1024, 1024], P(('blk', 'aux')), may hold values from -0.1875 to 0.1875
- three_centre: bfloat16 [1024, 32, 32, 1024], P(('blk', 'aux')), may hold values from -1 to 1
- occ_density: bfloat16 [256, 1024], P('blk'), may hold values from -1 to 1
- vir_density: bfloat16 [256, 1024], P('blk'), may hold values from -1 to 1
- block_sizes: int32 [256], P('blk'), may hold values from 16 to 32
- tile_rows: int32 [1024], P(('blk', 'aux')), may hold values from 0 to 7
- col_owner: int32 [1024, 1], P(('blk', 'aux')), may hold values from 0 to 31; in each aligned block of 32 rows (0 to 31, 32 to 63, ...) at most 2 rows name the same one
- col_block: int32 [1024], P(('blk', 'aux')), may hold values from 0 to 7
Outputs:
- occ_grad: float32 [256, 1024], P(('blk', 'aux'))
- vir_grad: float32 [256, 1024], P(('blk', 'aux'))
The draws below stay inside these ranges and needn't reach their ends.
Inputs may be any that keep to these rules, and one draw needn't show every extreme that they name: `col_owner`: among the 32 tiles of one blk index (aligned blocks of 32 tiles), at most 2 name the same owner, and some blk index reaches 2.
All inputs are finite; a program needn't handle non-finite values.
Results may differ from the reference program's by a relative error of at most 0.0041.
Values may be sent and summed in bfloat16 or wider, within the bound.
No kernel may reach another device: no remote copies, remote signals or barrier semaphores. Data moves between devices by JAX's collectives and lax.ppermute only.
A program may use at most 128 MiB of HBM per device.

```python
import math
import jax
import jax.numpy as jnp
import numpy as np
from jax import lax

BS = 32
NAUX = 1024
BLK_DEV = 8
TILE_DEV = 4
TILES_ROW = 32
CAP = 2
NB = 256
NTILE = 1024
N_BLK = 32


def plant(values, stream_key, smallest, top_value):
    longest = values.shape.index(max(values.shape))
    spots = []
    for shift in (0, 1):
        where = [jax.random.randint(jax.random.fold_in(stream_key, axis), (), 0, length) for axis, length in enumerate(values.shape)]
        where[longest] = (where[longest] + shift) % values.shape[longest]
        spots.append(tuple(where))
    return values.at[spots[0]].set(smallest).at[spots[1]].set(top_value)


def block_scale(key, dims, shards, low, high):
    def one(axis_at, parts):
        heights = jax.random.uniform(jax.random.fold_in(jax.random.fold_in(key, 6), axis_at), (parts,), jnp.float32, low / len(shards), high / len(shards))
        return jnp.repeat(jnp.exp(heights), dims[axis_at] // parts).reshape((-1,) + (1,) * (len(dims) - axis_at - 1))

    level = one(*shards[0])
    for cut in shards[1:]:
        level = level * one(*cut)
    return level


def assign_block(rng, own, number, rows, amount, top, most, slope):
    order = jax.random.permutation(rng, amount)
    packed, ordinary = portions_of(amount, rows * top, most, slope, True), portions_of(amount, rows * top, most, slope, False)
    places = jnp.arange(amount)

    def named(tallies, rotation):
        used = int((tallies > 0).sum())
        fixed = max(1, used // 4)
        shifted = fixed + (places - fixed + rotation * (used - fixed)) % max(1, amount - fixed)
        return jnp.zeros((amount,), jnp.int32).at[order[jnp.where(places < fixed, places, shifted)]].set(jnp.asarray(tallies, jnp.int32))

    tallies = jnp.where(number % 4 == 0, named(packed, number // 4), named(ordinary, number - number // 4 - 1))
    mixed = jax.random.permutation(jax.random.fold_in(own, 3), amount)
    source_of, taker = mixed[0:amount // 2 * 2:2], mixed[1:amount // 2 * 2:2]
    slack = jnp.minimum(tallies[source_of] - 1, most - tallies[taker]) // 2
    slack = jnp.where((source_of == order[0]) | (taker == order[0]) | (tallies[taker] == 0), 0, jnp.maximum(slack, 0))
    shifted = jax.random.randint(jax.random.fold_in(own, 4), (amount // 2,), 0, 1 << 20) % (slack + 1)
    tallies = tallies.at[source_of].add(-shifted).at[taker].add(shifted)
    items = jnp.searchsorted(jnp.cumsum(tallies), jnp.arange(rows * top), side="right").astype(jnp.int32)
    listing = items.reshape(top, rows).T
    listing = listing[jax.random.permutation(jax.random.fold_in(own, 1), rows)]
    rotation = jax.random.randint(jax.random.fold_in(own, 2), (rows, 1), 0, top)
    return jnp.take_along_axis(listing, (jnp.arange(top)[None, :] + rotation) % top, axis=1)


def portions_of(count, total, limit, slope, full):
    portions = [(1 << 20) // math.isqrt(rank ** slope) + 1 for rank in range(1, count + 1)]
    largest = limit if full else min(limit, max(-(-total // count), total * portions[0] // sum(portions)))
    least = 1 if total - largest >= count - 1 else 0
    counts, spare = [largest] + [least] * (count - 1), total - largest - least * (count - 1)
    while spare > 0:
        movable = [i for i in range(1, count) if counts[i] < largest] or [i for i in range(1, count) if counts[i] < limit]
        pool, budget = sum([portions[i] for i in movable]), spare
        for i in movable:
            extra = min(limit - counts[i], max(1, budget * portions[i] // pool), spare)
            counts[i] = counts[i] + extra
            spare = spare - extra
    return np.array(counts)


def bell_draw(stream_key, dims, width, bound, split=(), held_as=jnp.bfloat16):
    level = block_scale(stream_key, dims, split, -0.22, 0.18) if split else 1.0
    entries = jax.random.normal(stream_key, dims, jnp.float32) * width * level
    return jnp.minimum(jnp.maximum(entries, -bound), bound).astype(held_as)


def setup_inputs(seed: int = 0) -> dict:
    key_of = jax.random.split(jax.random.key(seed), 9)
    adjoint = bell_draw(key_of[0], (NAUX, NAUX), NAUX ** -0.5, 0.1875, ((0, 256),))
    three_centre = bell_draw(key_of[1], (NTILE, BS, BS, NAUX), BS ** -0.5, 1.0, ((0, 256),))
    occ_density = bell_draw(key_of[2], (NB, BS * BS), BS ** -0.5, 1.0, ((0, 32),))
    vir_density = bell_draw(key_of[3], (NB, BS * BS), BS ** -0.5, 1.0, ((0, 32),))
    block_sizes = plant(jax.random.randint(key_of[4], (NB,), BS // 2, BS + 1), jax.random.fold_in(key_of[4], 1), BS // 2, BS).astype(jnp.int32)
    tile_rows = plant(jax.random.randint(key_of[5], (NTILE,), 0, BLK_DEV), jax.random.fold_in(key_of[5], 1), 0, BLK_DEV - 1).astype(jnp.int32)
    col_owner_keys = jax.random.split(jax.random.fold_in(key_of[6], 1), NTILE // TILES_ROW)
    col_owner_turns = jax.random.permutation(jax.random.fold_in(key_of[6], 3), NTILE // TILES_ROW)
    col_owner = jax.vmap(lambda own, number: assign_block(jax.random.fold_in(key_of[6], 2), own, number, TILES_ROW, N_BLK, 1, CAP, 2))(col_owner_keys, col_owner_turns).reshape((NTILE, 1))
    col_block = plant(jax.random.randint(key_of[7], (NTILE,), 0, BLK_DEV), jax.random.fold_in(key_of[7], 1), 0, BLK_DEV - 1).astype(jnp.int32)
    return dict(adjoint=adjoint, three_centre=three_centre, occ_density=occ_density, vir_density=vir_density, block_sizes=block_sizes, tile_rows=tile_rows, col_owner=col_owner, col_block=col_block)


def reference(adjoint, three_centre, occ_density, vir_density, block_sizes, tile_rows, col_owner, col_block):
    func_index = jnp.arange(BS, dtype=jnp.int32)
    live_funcs = (func_index[None, :] < block_sizes[:, None]).astype(jnp.float32)
    live_pairs = (live_funcs[:, :, None] * live_funcs[:, None, :]).reshape(NB, BS * BS)
    occ_masked = (occ_density.astype(jnp.float32) * live_pairs).astype(jnp.bfloat16)
    vir_masked = (vir_density.astype(jnp.float32) * live_pairs).astype(jnp.bfloat16)
    tile_ids = jnp.arange(NTILE, dtype=jnp.int32)
    row_ids = ((tile_ids // TILES_ROW) * BLK_DEV + tile_rows).astype(jnp.int32)
    col_ids = (col_owner[:, 0] * BLK_DEV + col_block).astype(jnp.int32)
    adjoint_t = adjoint.T

    def one_group(totals, group_id):
        occ_acc, vir_acc = totals
        first = (group_id * TILE_DEV).astype(jnp.int32)
        tile_group = lax.dynamic_slice_in_dim(three_centre, first, TILE_DEV, 0)
        group_rows = lax.dynamic_slice_in_dim(row_ids, first, TILE_DEV, 0)
        group_cols = lax.dynamic_slice_in_dim(col_ids, first, TILE_DEV, 0)
        tile_flat = tile_group.reshape(TILE_DEV * BS * BS, NAUX)
        contracted = jnp.dot(tile_flat, adjoint_t, preferred_element_type=jnp.float32).astype(jnp.bfloat16)
        contracted = contracted.reshape(TILE_DEV, BS, BS, NAUX).astype(jnp.float32)
        vir_tile_d = vir_masked[group_cols].reshape(TILE_DEV, BS, BS).astype(jnp.float32)
        occ_tile_d = occ_masked[group_rows].reshape(TILE_DEV, BS, BS).astype(jnp.float32)
        tiles_f = tile_group.astype(jnp.float32)
        weighted = jnp.einsum('tjk,tijq->tikq', vir_tile_d, contracted).astype(jnp.bfloat16).astype(jnp.float32)
        occ_tile = jnp.einsum('tikq,tlkq->til', weighted, tiles_f)
        rotated = jnp.einsum('tij,tjkq->tikq', occ_tile_d, tiles_f).astype(jnp.bfloat16).astype(jnp.float32)
        vir_tile = jnp.einsum('tijq,tikq->tjk', contracted, rotated)
        occ_acc = occ_acc.at[group_rows].add(occ_tile.reshape(TILE_DEV, BS * BS))
        vir_acc = vir_acc.at[group_cols].add(vir_tile.reshape(TILE_DEV, BS * BS))
        return (occ_acc, vir_acc), None

    zeros = jnp.zeros((NB, BS * BS), jnp.float32)
    (occ_acc, vir_acc), _ = lax.scan(one_group, (zeros, zeros), jnp.arange(NTILE // TILE_DEV, dtype=jnp.int32))
    norm_factor = NAUX ** -0.5
    return occ_acc * live_pairs * norm_factor, vir_acc * live_pairs * norm_factor
```

```python
import functools
import jax
import jax.numpy as jnp
from jax import lax
from jax.experimental import pallas as pl
from jax.experimental.pallas import tpu as pltpu
from jax.sharding import Mesh, PartitionSpec as P

BS = 32
NAUX = 1024
HALF = 640
NZ, NY, NX, NC = 8, 4, 4, 2
TILES = 4
BLOCKS = 8
F32 = jnp.float32
BF16 = jnp.bfloat16
NORM = NAUX ** -0.5
PAY = NAUX + 128
ANY = pl.BlockSpec(memory_space=pl.ANY)
SMEM = pl.BlockSpec(memory_space=pltpu.SMEM)
VMEM = pl.BlockSpec(memory_space=pltpu.VMEM)


def dot(a, b, ca, cb):
    return lax.dot_general(a, b, (((ca,), (cb,)), ((), ())), preferred_element_type=F32)


def iota(shape, dim):
    return lax.broadcasted_iota(jnp.int32, shape, dim)


def pair_mask(size):
    lane = iota((1, NAUX), 1)
    return ((lane // BS < size) & (lane % BS < size)).astype(F32)


def pick_row(block, row):
    return jnp.sum(jnp.where(iota(block.shape, 0) == row, block.astype(F32), 0.0), axis=0, keepdims=True)


def prepare_kernel(sizes, adj_ref, vir_ref, out_ref):
    aux = lax.axis_index("x") * NC + lax.axis_index("c")
    row = (pick_row(vir_ref[...], aux) * pair_mask(sizes[aux])).astype(BF16)
    quarters = jnp.concatenate([row[:, 256 * r : 256 * (r + 1)] for r in range(4)], axis=0)
    for c in range(NC):
        share = jnp.concatenate(
            [adj_ref[:, 512 * c : 512 * (c + 1)], quarters[:, 128 * c : 128 * (c + 1)]], axis=1
        )
        out_ref[:, c] = jnp.broadcast_to(share[None], (NZ * NX, 4, HALF))


def tile_kernel(
    rows, owners, blocks, sizes, tile_ref, occ_ref,
    m0, m1, m2, m3, s0, s1, s2, s3, pay_ref,
    adj, vir, g_ref, ct_ref, oexp, vexp, vacc, oacc, pay, occ_sum, sem,
):
    t = pl.program_id(0)
    y = lax.axis_index("y")
    c = lax.axis_index("c")
    width = 256
    chunks = NAUX // width

    def copies():
        found = []
        for half, group in ((c, (m0, m1, m2, m3)), (1 - c, (s0, s1, s2, s3))):
            for shift, src in enumerate(group):
                at = lax.rem(y + NY - shift, NY)
                n = len(found)
                found.append(pltpu.make_async_copy(
                    src.at[:, :, pl.ds(0, 512)],
                    adj.at[:, at, :, pl.ds(pl.multiple_of(half * 512, 512), 512)], sem.at[n]))
                found.append(pltpu.make_async_copy(
                    src.at[:, :, pl.ds(512, 128)],
                    vir.at[:, at, :, pl.ds(pl.multiple_of(half * 128, 128), 128)], sem.at[n + 1]))
        return found

    @pl.when(t == 0)
    def _():
        for copy in copies():
            copy.start()
        pay[...] = jnp.zeros_like(pay)
        pay[:, :, NAUX:] = jnp.full((BLOCKS, 8, 128), -1.0, F32)
        occ_sum[...] = jnp.zeros_like(occ_sum)
        for copy in copies():
            copy.wait()

    r = rows[t]
    owner = owners[t, 0]
    block = blocks[t]
    occ_row = pick_row(occ_ref[...], r) * pair_mask(sizes[r])
    occ_sel = jnp.where(iota((BS, NAUX), 0) == iota((BS, NAUX), 1) % BS, occ_row, 0.0).astype(BF16)
    same = (iota((128, 128), 0) // BS == iota((128, 128), 1) // BS).astype(BF16)
    for m in range(8):
        lanes = slice(128 * m, 128 * (m + 1))
        oexp[:, lanes] = dot(occ_sel[:, lanes], same, 1, 0)
    col = owner * BLOCKS + block
    sub = lax.rem(col, 8)
    z_at = col // 32
    y_at = lax.rem(col // 8, NY)
    v32 = vir[z_at, y_at]
    pick = (iota((BS, BS), 1) == sub * 4 + iota((BS, BS), 0) // 8).astype(BF16)
    spread = dot(pick, v32, 1, 0)
    spread = jnp.where(iota((BS, 256), 1) // BS == iota((BS, 256), 0) % 8, spread, 0.0).astype(BF16)
    fold = (iota((256, BS), 0) % BS == iota((256, BS), 1)).astype(BF16)
    v_block = dot(spread, fold, 1, 0).astype(BF16)
    repeat = (iota((BS, NAUX), 0) == iota((BS, NAUX), 1) % BS).astype(BF16)
    vexp[...] = dot(v_block, repeat, 0, 0)

    def contract(n):
        a = adj[...].reshape(NAUX, NAUX)
        ct_ref[n % 2] = dot(a, tile_ref[0, n * width : (n + 1) * width, :], 1, 1).astype(BF16)

    def gram(n):
        g_ref[n % 2] = dot(tile_ref[0], ct_ref[n % 2], 1, 0)

    def reduce(n):
        lanes = slice(n * width, (n + 1) * width)
        vx = vexp[:, lanes]
        acc = jnp.zeros((BS, width), F32)
        for l in range(BS):
            g = g_ref[n % 2, l * BS : (l + 1) * BS, :]
            acc = acc + oexp[l : l + 1, lanes] * g
            oacc[l : l + 1, lanes] = jnp.sum(vx * g, axis=0, keepdims=True)
        vacc[:, lanes] = acc

    contract(0)
    for n in range(chunks):
        if n + 1 < chunks:
            contract(n + 1)
        if n > 0:
            reduce(n - 1)
        gram(n)
    reduce(chunks - 1)

    va = vacc[...]
    virt = va[:, :128]
    for m in range(1, 8):
        virt = virt + va[:, m * 128 : (m + 1) * 128]
    virt = virt + pltpu.roll(virt, 64, 1)
    virt = virt + pltpu.roll(virt, 32, 1)
    oa = oacc[...]
    high = oa.astype(BF16)
    rest = oa - high.astype(F32)
    mid = rest.astype(BF16)
    low = (rest - mid.astype(F32)).astype(BF16)
    group = (iota((NAUX, 128), 0) // BS == iota((NAUX, 128), 1) % BS).astype(BF16)
    occt = dot(high, group, 1, 0) + dot(mid, group, 1, 0) + dot(low, group, 1, 0)

    def flat(x):
        x = jnp.concatenate([x] * 4, axis=0).T[:BS]
        x = jnp.concatenate([x] * 8, axis=1)
        x = jnp.where(iota((BS, NAUX), 0) == iota((BS, NAUX), 1) // BS, x, 0.0)
        return jnp.sum(x, axis=0, keepdims=True)

    dest = iota((BLOCKS, NAUX), 0)
    occ_sum[...] += jnp.where(dest == r, flat(occt), 0.0)
    mine = jnp.where(dest == block, flat(virt), 0.0)
    label = jnp.where(iota((BLOCKS, 128), 0) == block, owner.astype(F32), -1.0)
    whole = jnp.concatenate([mine, label], axis=1)
    pay[...] = jnp.where(iota((BLOCKS, 8, PAY), 1) == t, whole[:, None, :], pay[...])

    @pl.when(t == TILES - 1)
    def _():
        total = occ_sum[...]
        top = total.astype(BF16).astype(F32)
        pay[:, 4:5, :NAUX] = top[:, None, :]
        pay[:, 5:6, :NAUX] = (total - top)[:, None, :]
        pay_ref[...] = pay[...].astype(BF16)


def route_kernel(sizes, got_ref, occ_ref, out_ref, spread):
    aux = lax.axis_index("x") * NC + lax.axis_index("c")
    got = got_ref[...].astype(F32)
    occ = jnp.sum(got[:, 4, :NAUX] + got[:, 5, :NAUX], axis=0, keepdims=True)
    occ_ref[...] = occ * pair_mask(sizes[aux]) * NORM
    flat = got.reshape(8 * BLOCKS, PAY)
    hot = (flat[:, NAUX:] == iota((8 * BLOCKS, 128), 1).astype(F32)).astype(BF16)
    terms = dot(hot, flat[:, :NAUX].astype(BF16), 0, 0)[: NZ * NY]
    for s in range(8):
        spread[:, s, :] = terms[:, 128 * s : 128 * (s + 1)]
    out_ref[...] = spread[...].astype(BF16)


def finish_kernel(sizes, got_ref, out_ref):
    aux = lax.axis_index("x") * NC + lax.axis_index("c")
    total = jnp.sum(got_ref[...].astype(F32), axis=0)
    row = jnp.concatenate([total[s : s + 1] for s in range(8)], axis=1)
    out_ref[...] = row * pair_mask(sizes[aux]) * NORM


def shards(adjoint, three_centre, occ_density, vir_density, block_sizes, tile_rows, col_owner, col_block):
    tiles = three_centre.reshape(TILES, BS * BS, NAUX)
    share = pl.pallas_call(
        prepare_kernel,
        out_shape=jax.ShapeDtypeStruct((NZ * NX, NC, 4, HALF), BF16),
        in_specs=[SMEM, VMEM, VMEM],
        out_specs=VMEM,
        name="prepare",
    )(block_sizes, adjoint, vir_density)
    share = share.reshape(NZ * NX * NC, 4, HALF)
    own = lax.all_to_all(share, ("z", "x", "c"), 0, 0, tiled=True).reshape(NZ, 32, HALF)
    mine = [own] + [
        lax.ppermute(own, "y", [(i, (i + s) % NY) for i in range(NY)]) for s in (1, 2, 3)
    ]
    other = [lax.ppermute(m, "c", [(0, 1), (1, 0)]) for m in mine]
    pay = pl.pallas_call(
        tile_kernel,
        grid_spec=pltpu.PrefetchScalarGridSpec(
            num_scalar_prefetch=4,
            grid=(TILES,),
            in_specs=[
                pl.BlockSpec((1, NAUX, NAUX), lambda t, *_: (t, 0, 0)),
                pl.BlockSpec((BLOCKS, NAUX), lambda t, *_: (0, 0), pipeline_mode=pl.Buffered(1)),
            ] + [ANY] * 8,
            out_specs=pl.BlockSpec((BLOCKS, 8, PAY), lambda t, *_: (0, 0, 0)),
            scratch_shapes=[
                pltpu.VMEM((NZ, NY, 32, NAUX), BF16),
                pltpu.VMEM((NZ, NY, 32, 256), BF16),
                pltpu.VMEM((2, NAUX, 256), F32),
                pltpu.VMEM((2, NAUX, 256), BF16),
                pltpu.VMEM((BS, NAUX), F32),
                pltpu.VMEM((BS, NAUX), F32),
                pltpu.VMEM((BS, NAUX), F32),
                pltpu.VMEM((BS, NAUX), F32),
                pltpu.VMEM((BLOCKS, 8, PAY), F32),
                pltpu.VMEM((BLOCKS, NAUX), F32),
                pltpu.SemaphoreType.DMA((16,)),
            ],
        ),
        out_shape=jax.ShapeDtypeStruct((BLOCKS, 8, PAY), BF16),
        compiler_params=pltpu.CompilerParams(
            vmem_limit_bytes=40 << 20, dimension_semantics=("arbitrary",)
        ),
        name="tiles",
    )(tile_rows, col_owner, col_block, block_sizes, tiles, occ_density, *mine, *other)
    got = lax.all_to_all(pay, ("x", "c"), 0, 0, tiled=True)
    occ_grad, terms = pl.pallas_call(
        route_kernel,
        out_shape=(
            jax.ShapeDtypeStruct((1, NAUX), F32),
            jax.ShapeDtypeStruct((NZ * NY, 8, 128), BF16),
        ),
        in_specs=[SMEM, VMEM],
        out_specs=(VMEM, VMEM),
        scratch_shapes=[pltpu.VMEM((NZ * NY, 8, 128), F32)],
        name="route",
    )(block_sizes, got)
    back = lax.all_to_all(terms, ("z", "y"), 0, 0, tiled=True)
    vir_grad = pl.pallas_call(
        finish_kernel,
        out_shape=jax.ShapeDtypeStruct((1, NAUX), F32),
        in_specs=[SMEM, VMEM],
        out_specs=VMEM,
        name="finish",
    )(block_sizes, back)
    return occ_grad, vir_grad


def solution(mesh):
    grid = Mesh(mesh.devices.reshape(NZ, NY, NX, NC), ("z", "y", "x", "c"))
    every = ("z", "y", "x", "c")
    blk = ("z", "y")
    in_specs = (
        P(every, None),
        P(every, None, None, None),
        P(blk, None),
        P(blk, None),
        P(blk),
        P(every),
        P(every, None),
        P(every),
    )
    out_specs = (P(every, None), P(every, None))
    return jax.shard_map(shards, mesh=grid, in_specs=in_specs, out_specs=out_specs, check_vma=False)
```

```python
import functools
import jax
import jax.numpy as jnp
from jax import lax
from jax.experimental import pallas as pl
from jax.experimental.pallas import tpu as pltpu
from jax.sharding import Mesh, PartitionSpec as P

BS = 32
NAUX = 1024
HALF = 640
NZ, NY, NX, NC = 8, 4, 4, 2
TILES = 4
BLOCKS = 8
F32 = jnp.float32
BF16 = jnp.bfloat16
NORM = NAUX ** -0.5
PAY = NAUX + 128
ANY = pl.BlockSpec(memory_space=pl.ANY)
SMEM = pl.BlockSpec(memory_space=pltpu.SMEM)
VMEM = pl.BlockSpec(memory_space=pltpu.VMEM)


def dot(a, b, ca, cb):
    return lax.dot_general(a, b, (((ca,), (cb,)), ((), ())), preferred_element_type=F32)


def iota(shape, dim):
    return lax.broadcasted_iota(jnp.int32, shape, dim)


def pair_mask(size):
    lane = iota((1, NAUX), 1)
    return ((lane // BS < size) & (lane % BS < size)).astype(F32)


def pick_row(block, row):
    return jnp.sum(jnp.where(iota(block.shape, 0) == row, block.astype(F32), 0.0), axis=0, keepdims=True)


def prepare_kernel(sizes, adj_ref, vir_ref, out_ref):
    aux = lax.axis_index("x") * NC + lax.axis_index("c")
    row = (pick_row(vir_ref[...], aux) * pair_mask(sizes[aux])).astype(BF16)
    quarters = jnp.concatenate([row[:, 256 * r : 256 * (r + 1)] for r in range(4)], axis=0)
    for c in range(NC):
        share = jnp.concatenate(
            [adj_ref[:, 512 * c : 512 * (c + 1)], quarters[:, 128 * c : 128 * (c + 1)]], axis=1
        )
        out_ref[:, c] = jnp.broadcast_to(share[None], (NZ * NX, 4, HALF))


def chunk_slots(y):
    return [lax.rem(y + NY - shift, NY) for shift in (0, 1, 3, 2)]


def half_lanes(half, width):
    return pl.ds(pl.multiple_of(half * width, width), width)


def contract_kernel(count, tile_ref, *refs):
    mine, other = refs[:count], refs[count : 2 * count]
    outs = refs[2 * count + 1 : 3 * count + 1]
    token, adj, sem = refs[3 * count + 1 :]
    c = lax.axis_index("c")

    def copies():
        found = []
        for half, group in ((c, mine), (1 - c, other)):
            for m, src in enumerate(group):
                found.append(pltpu.make_async_copy(
                    src.at[:, :, pl.ds(0, 512)], adj.at[m, :, :, half_lanes(half, 512)], sem.at[len(found)]))
        return found

    @pl.when(pl.program_id(0) == 0)
    def _():
        for copy in copies():
            copy.start()
        token[...] = jnp.zeros_like(token)
        for copy in copies():
            copy.wait()

    for m in range(count):
        a = adj[m].reshape(256, NAUX)
        for n in range(4):
            lanes = slice(256 * n, 256 * (n + 1))
            outs[m][0, :, :, lanes] = dot(a, tile_ref[0, lanes, :], 1, 1).astype(BF16).reshape(NZ, 32, 256)


def in_hbm(x):
    return pltpu.with_memory_space_constraint(x, pltpu.HBM)


def contract(tiles, mine, other, after, name):
    count = len(mine)
    return pl.pallas_call(
        functools.partial(contract_kernel, count),
        grid=(TILES,),
        in_specs=[pl.BlockSpec((1, NAUX, NAUX), lambda t: (t, 0, 0))] + [ANY] * (2 * count + 1),
        out_specs=[pl.BlockSpec((1, NZ, 32, NAUX), lambda t: (t, 0, 0, 0))] * count
        + [pl.BlockSpec((8, 128), lambda t: (0, 0))],
        out_shape=[jax.ShapeDtypeStruct((TILES, NZ, 32, NAUX), BF16)] * count
        + [jax.ShapeDtypeStruct((8, 128), F32)],
        scratch_shapes=[
            pltpu.VMEM((count, NZ, 32, NAUX), BF16),
            pltpu.SemaphoreType.DMA((2 * count,)),
        ],
        compiler_params=pltpu.CompilerParams(vmem_limit_bytes=20 << 20),
        cost_estimate=pl.CostEstimate(
            flops=2 * count * TILES * NAUX * NAUX * 256, bytes_accessed=(8 + 2 * count) << 20, transcendentals=0
        ),
        name=name,
    )(in_hbm(tiles), *mine, *other, after)


def tile_kernel(
    tile_ref, occ_ref, rows_h, owners_h, blocks_h, sizes_h,
    m0, m1, m3, s0, s1, s3, m2a, m2b, s2a, s2b, c0, c1, c3, after, pay_ref,
    adj, vir, ct, g_ref, oexp, vexp, vacc, oacc, pay, occ_sum,
    rows, owners, blocks, sizes, sem, ct_sem, s_sem,
):
    t = pl.program_id(0)
    y = lax.axis_index("y")
    c = lax.axis_index("c")
    slots = chunk_slots(y)
    width = 256
    chunks = NAUX // width

    def scalars():
        pairs = ((rows_h, rows), (owners_h, owners), (blocks_h, blocks), (sizes_h, sizes))
        return [pltpu.make_async_copy(src, dst, s_sem.at[n]) for n, (src, dst) in enumerate(pairs)]

    def gathered():
        found = []

        def add(src, dst):
            found.append(pltpu.make_async_copy(src, dst, sem.at[len(found)]))

        for half, group, last in ((c, (m0, m1, m3), (m2a, m2b)), (1 - c, (s0, s1, s3), (s2a, s2b))):
            for src, at in zip(group, slots):
                add(src.at[:, :, pl.ds(512, 128)], vir.at[:, at, :, half_lanes(half, 128)])
            for n, src in enumerate(last):
                part = pl.ds(n * (NZ // 2), NZ // 2)
                add(src.at[:, :, pl.ds(512, 128)], vir.at[part, slots[3], :, half_lanes(half, 128)])
                add(src.at[:, :, pl.ds(0, 512)], adj.at[part, :, half_lanes(half, 512)])
        return found

    def contracted(tile):
        b = lax.rem(tile, 2)
        return [
            pltpu.make_async_copy(src.at[tile], ct.at[b, :, at], ct_sem.at[b, n])
            for n, (src, at) in enumerate(zip((c0, c1, c3), slots))
        ]

    @pl.when(t == 0)
    def _():
        for copy in scalars() + gathered() + contracted(0):
            copy.start()
        pay[...] = jnp.zeros_like(pay)
        pay[:, :, NAUX:] = jnp.full((BLOCKS, 8, 128), -1.0, F32)
        occ_sum[...] = jnp.zeros_like(occ_sum)
        for copy in scalars() + gathered():
            copy.wait()

    @pl.when(t + 1 < TILES)
    def _():
        for copy in contracted(t + 1):
            copy.start()

    @pl.when(t < TILES)
    def _():
        for copy in contracted(t):
            copy.wait()

    def reduce(n):
        lanes = slice(n * width, (n + 1) * width)
        vx = vexp[:, lanes]
        acc = jnp.zeros((BS, width), F32)
        for l in range(BS):
            g = g_ref[n % 2, l * BS : (l + 1) * BS, :]
            acc = acc + oexp[l : l + 1, lanes] * g
            oacc[l : l + 1, lanes] = jnp.sum(vx * g, axis=0, keepdims=True)
        vacc[:, lanes] = acc

    def flat(x):
        x = jnp.concatenate([x] * 4, axis=0).T[:BS]
        x = jnp.concatenate([x] * 8, axis=1)
        x = jnp.where(iota((BS, NAUX), 0) == iota((BS, NAUX), 1) // BS, x, 0.0)
        return jnp.sum(x, axis=0, keepdims=True)

    def collect(tile, valid):
        va = vacc[...]
        virt = va[:, :128]
        for m in range(1, 8):
            virt = virt + va[:, m * 128 : (m + 1) * 128]
        virt = virt + pltpu.roll(virt, 64, 1)
        virt = virt + pltpu.roll(virt, 32, 1)
        oa = oacc[...]
        high = oa.astype(BF16)
        rest = oa - high.astype(F32)
        mid = rest.astype(BF16)
        low = (rest - mid.astype(F32)).astype(BF16)
        group = (iota((NAUX, 128), 0) // BS == iota((NAUX, 128), 1) % BS).astype(BF16)
        occt = dot(high, group, 1, 0) + dot(mid, group, 1, 0) + dot(low, group, 1, 0)
        block = blocks[tile]
        dest = iota((BLOCKS, NAUX), 0)
        occ_sum[...] += jnp.where((dest == rows[tile]) & valid, flat(occt), 0.0)
        mine = jnp.where(dest == block, flat(virt), 0.0)
        label = jnp.where(iota((BLOCKS, 128), 0) == block, owners[tile].astype(F32), -1.0)
        whole = jnp.concatenate([mine, label], axis=1)
        pay[...] = jnp.where((iota((BLOCKS, 8, PAY), 1) == tile) & valid, whole[:, None, :], pay[...])

    @pl.when(t < TILES)
    def _():
        reduce(chunks - 1)
        b = lax.rem(t, 2)
        a = adj[...].reshape(256, NAUX)
        for n in range(chunks):
            lanes = slice(n * width, (n + 1) * width)
            ct[b, :, slots[3], :, lanes] = dot(a, tile_ref[0, lanes, :], 1, 1).astype(BF16).reshape(NZ, 32, width)
        collect(jnp.maximum(t - 1, 0), t > 0)
        r = rows[t]
        occ_row = pick_row(occ_ref[...], r) * pair_mask(sizes[r])
        occ_sel = jnp.where(iota((BS, NAUX), 0) == iota((BS, NAUX), 1) % BS, occ_row, 0.0).astype(BF16)
        same = (iota((128, 128), 0) // BS == iota((128, 128), 1) // BS).astype(BF16)
        for m in range(8):
            lanes = slice(128 * m, 128 * (m + 1))
            oexp[:, lanes] = dot(occ_sel[:, lanes], same, 1, 0)
        col = owners[t] * BLOCKS + blocks[t]
        v32 = vir[col // 32, lax.rem(col // 8, NY)]
        pick = (iota((BS, BS), 1) == lax.rem(col, 8) * 4 + iota((BS, BS), 0) // 8).astype(BF16)
        spread = dot(pick, v32, 1, 0)
        spread = jnp.where(iota((BS, 256), 1) // BS == iota((BS, 256), 0) % 8, spread, 0.0).astype(BF16)
        fold = (iota((256, BS), 0) % BS == iota((256, BS), 1)).astype(BF16)
        v_block = dot(spread, fold, 1, 0).astype(BF16)
        repeat = (iota((BS, NAUX), 0) == iota((BS, NAUX), 1) % BS).astype(BF16)
        vexp[...] = dot(v_block, repeat, 0, 0)
        for n in range(chunks):
            lanes = slice(n * width, (n + 1) * width)
            if n > 0:
                g_ref[n % 2] = dot(tile_ref[0], ct[b, :, :, :, lanes].reshape(NAUX, width), 1, 0)
                reduce(n - 1)
            else:
                g_ref[0] = dot(tile_ref[0], ct[b, :, :, :, lanes].reshape(NAUX, width), 1, 0)

    @pl.when(t == TILES)
    def _():
        reduce(chunks - 1)
        collect(TILES - 1, True)
        total = occ_sum[...]
        top = total.astype(BF16).astype(F32)
        pay[:, 4:5, :NAUX] = top[:, None, :]
        pay[:, 5:6, :NAUX] = (total - top)[:, None, :]
        pay_ref[...] = pay[...].astype(BF16)


def route_kernel(sizes, got_ref, occ_ref, out_ref, spread):
    aux = lax.axis_index("x") * NC + lax.axis_index("c")
    got = got_ref[...].astype(F32)
    occ = jnp.sum(got[:, 4, :NAUX] + got[:, 5, :NAUX], axis=0, keepdims=True)
    occ_ref[...] = occ * pair_mask(sizes[aux]) * NORM
    flat = got.reshape(8 * BLOCKS, PAY)
    hot = (flat[:, NAUX:] == iota((8 * BLOCKS, 128), 1).astype(F32)).astype(BF16)
    terms = dot(hot, flat[:, :NAUX].astype(BF16), 0, 0)[: NZ * NY]
    for s in range(8):
        spread[:, s, :] = terms[:, 128 * s : 128 * (s + 1)]
    out_ref[...] = spread[...].astype(BF16)


def finish_kernel(sizes, got_ref, out_ref):
    aux = lax.axis_index("x") * NC + lax.axis_index("c")
    total = jnp.sum(got_ref[...].astype(F32), axis=0)
    row = jnp.concatenate([total[s : s + 1] for s in range(8)], axis=1)
    out_ref[...] = row * pair_mask(sizes[aux]) * NORM


def shards(adjoint, three_centre, occ_density, vir_density, block_sizes, tile_rows, col_owner, col_block):
    tiles = three_centre.reshape(TILES, BS * BS, NAUX)
    share = pl.pallas_call(
        prepare_kernel,
        out_shape=jax.ShapeDtypeStruct((NZ * NX, NC, 4, HALF), BF16),
        in_specs=[SMEM, VMEM, VMEM],
        out_specs=VMEM,
        name="prepare",
    )(block_sizes, adjoint, vir_density)
    share = share.reshape(NZ * NX * NC, 4, HALF)
    own = lax.all_to_all(share, ("z", "x", "c"), 0, 0, tiled=True).reshape(NZ, 32, HALF)
    ahead = [(i, (i + 1) % NY) for i in range(NY)]
    behind = [(i, (i - 1) % NY) for i in range(NY)]

    def sibling(x):
        return lax.ppermute(x, "c", [(0, 1), (1, 0)])

    def shift(x, pairs):
        return lax.ppermute(x, "y", pairs)

    m1 = shift(own, ahead)
    m3 = shift(own, behind)
    s0 = sibling(own)
    c0, token = contract(tiles, [own], [s0], own, "contract_own")
    m1, m3, token = lax.optimization_barrier((m1, m3, token))
    m2a = shift(m1[: NZ // 2], ahead)
    m2b = shift(m3[NZ // 2 :], behind)
    s1 = sibling(m1)
    s3 = sibling(m3)
    c1, c3, token = contract(tiles, [m1, m3], [s1, s3], token, "contract_sides")
    m2a, m2b, token = lax.optimization_barrier((m2a, m2b, token))
    s2a = sibling(m2a)
    s2b = sibling(m2b)

    pay = pl.pallas_call(
        tile_kernel,
        grid=(TILES + 1,),
        in_specs=[
            pl.BlockSpec((1, NAUX, NAUX), lambda t: (jnp.minimum(t, TILES - 1), 0, 0)),
            pl.BlockSpec((BLOCKS, NAUX), lambda t: (0, 0), pipeline_mode=pl.Buffered(1)),
        ] + [ANY] * 18,
        out_specs=pl.BlockSpec((BLOCKS, 8, PAY), lambda t: (0, 0, 0)),
        scratch_shapes=[
            pltpu.VMEM((NZ, 32, NAUX), BF16),
            pltpu.VMEM((NZ, NY, 32, 256), BF16),
            pltpu.VMEM((2, NZ, NY, 32, NAUX), BF16),
            pltpu.VMEM((2, NAUX, 256), F32),
            pltpu.VMEM((BS, NAUX), F32),
            pltpu.VMEM((BS, NAUX), F32),
            pltpu.VMEM((BS, NAUX), F32),
            pltpu.VMEM((BS, NAUX), F32),
            pltpu.VMEM((BLOCKS, 8, PAY), F32),
            pltpu.VMEM((BLOCKS, NAUX), F32),
            pltpu.SMEM((TILES,), jnp.int32),
            pltpu.SMEM((TILES,), jnp.int32),
            pltpu.SMEM((TILES,), jnp.int32),
            pltpu.SMEM((BLOCKS,), jnp.int32),
            pltpu.SemaphoreType.DMA((14,)),
            pltpu.SemaphoreType.DMA((2, 3)),
            pltpu.SemaphoreType.DMA((4,)),
        ],
        out_shape=jax.ShapeDtypeStruct((BLOCKS, 8, PAY), BF16),
        compiler_params=pltpu.CompilerParams(vmem_limit_bytes=24 << 20),
        cost_estimate=pl.CostEstimate(flops=11 << 30, bytes_accessed=16 << 20, transcendentals=0),
        name="tiles",
    )(
        *map(in_hbm, (tiles, occ_density, tile_rows, col_owner.reshape(TILES), col_block, block_sizes)),
        own, m1, m3, s0, s1, s3, m2a, m2b, s2a, s2b, c0, c1, c3, token,
    )
    got = lax.all_to_all(pay, ("x", "c"), 0, 0, tiled=True)
    occ_grad, terms = pl.pallas_call(
        route_kernel,
        out_shape=(
            jax.ShapeDtypeStruct((1, NAUX), F32),
            jax.ShapeDtypeStruct((NZ * NY, 8, 128), BF16),
        ),
        in_specs=[SMEM, VMEM],
        out_specs=(VMEM, VMEM),
        scratch_shapes=[pltpu.VMEM((NZ * NY, 8, 128), F32)],
        name="route",
    )(block_sizes, got)
    back = lax.all_to_all(terms, ("z", "y"), 0, 0, tiled=True)
    vir_grad = pl.pallas_call(
        finish_kernel,
        out_shape=jax.ShapeDtypeStruct((1, NAUX), F32),
        in_specs=[SMEM, VMEM],
        out_specs=VMEM,
        name="finish",
    )(block_sizes, back)
    return occ_grad, vir_grad


def solution(mesh):
    grid = Mesh(mesh.devices.reshape(NZ, NY, NX, NC), ("z", "y", "x", "c"))
    every = ("z", "y", "x", "c")
    blk = ("z", "y")
    in_specs = (
        P(every, None),
        P(every, None, None, None),
        P(blk, None),
        P(blk, None),
        P(blk),
        P(every),
        P(every, None),
        P(every),
    )
    out_specs = (P(every, None), P(every, None))
    return jax.shard_map(shards, mesh=grid, in_specs=in_specs, out_specs=out_specs, check_vma=False)
```

```python
import functools
import jax
import jax.numpy as jnp
from jax import lax
from jax.experimental import pallas as pl
from jax.experimental.pallas import tpu as pltpu
from jax.sharding import Mesh, PartitionSpec as P

BS = 32
NAUX = 1024
HALF = 640
NZ, NY, NX, NC = 8, 4, 4, 2
TILES = 4
BLOCKS = 8
F32 = jnp.float32
BF16 = jnp.bfloat16
NORM = NAUX ** -0.5
PAY = NAUX + 128
ANY = pl.BlockSpec(memory_space=pl.ANY)
SMEM = pl.BlockSpec(memory_space=pltpu.SMEM)
VMEM = pl.BlockSpec(memory_space=pltpu.VMEM)


def dot(a, b, ca, cb):
    return lax.dot_general(a, b, (((ca,), (cb,)), ((), ())), preferred_element_type=F32)


def iota(shape, dim):
    return lax.broadcasted_iota(jnp.int32, shape, dim)


def pair_mask(size):
    lane = iota((1, NAUX), 1)
    return ((lane // BS < size) & (lane % BS < size)).astype(F32)


def pick_row(block, row):
    return jnp.sum(jnp.where(iota(block.shape, 0) == row, block.astype(F32), 0.0), axis=0, keepdims=True)


def prepare_kernel(sizes, adj_ref, vir_ref, out_ref):
    aux = lax.axis_index("x") * NC + lax.axis_index("c")
    row = (pick_row(vir_ref[...], aux) * pair_mask(sizes[aux])).astype(BF16)
    quarters = jnp.concatenate([row[:, 256 * r : 256 * (r + 1)] for r in range(4)], axis=0)
    for c in range(NC):
        share = jnp.concatenate(
            [adj_ref[:, 512 * c : 512 * (c + 1)], quarters[:, 128 * c : 128 * (c + 1)]], axis=1
        )
        out_ref[:, c] = jnp.broadcast_to(share[None], (NZ * NX, 4, HALF))


def chunk_slots(y):
    return [lax.rem(y + NY - shift, NY) for shift in (0, 1, 3, 2)]


def half_lanes(half, width):
    return pl.ds(pl.multiple_of(half * width, width), width)


def contract_kernel(count, tile_ref, *refs):
    mine, other = refs[:count], refs[count : 2 * count]
    outs = refs[2 * count + 1 : 3 * count + 1]
    token, adj, sem = refs[3 * count + 1 :]
    c = lax.axis_index("c")

    def copies():
        found = []
        for half, group in ((c, mine), (1 - c, other)):
            for m, src in enumerate(group):
                found.append(pltpu.make_async_copy(
                    src.at[:, :, pl.ds(0, 512)], adj.at[m, :, :, half_lanes(half, 512)], sem.at[len(found)]))
        return found

    @pl.when(pl.program_id(0) == 0)
    def _():
        for copy in copies():
            copy.start()
        token[...] = jnp.zeros_like(token)
        for copy in copies():
            copy.wait()

    t = pl.program_id(0)
    for m in range(count):
        a = adj[m].reshape(256, NAUX)
        for n in range(4):
            lanes = slice(256 * n, 256 * (n + 1))
            outs[m][0, :, :, lanes] = dot(a, tile_ref[t, lanes, :], 1, 1).astype(BF16).reshape(NZ, 32, 256)


def in_hbm(x):
    return pltpu.with_memory_space_constraint(x, pltpu.HBM)


def in_vmem(x):
    return pltpu.with_memory_space_constraint(x, pltpu.VMEM)


def contract(tiles, mine, other, after, name):
    count = len(mine)
    return pl.pallas_call(
        functools.partial(contract_kernel, count),
        grid=(TILES,),
        in_specs=[VMEM] + [ANY] * (2 * count + 1),
        out_specs=[pl.BlockSpec((1, NZ, 32, NAUX), lambda t: (t, 0, 0, 0))] * count
        + [pl.BlockSpec((8, 128), lambda t: (0, 0))],
        out_shape=[jax.ShapeDtypeStruct((TILES, NZ, 32, NAUX), BF16)] * count
        + [jax.ShapeDtypeStruct((8, 128), F32)],
        scratch_shapes=[
            pltpu.VMEM((count, NZ, 32, NAUX), BF16),
            pltpu.SemaphoreType.DMA((2 * count,)),
        ],
        compiler_params=pltpu.CompilerParams(vmem_limit_bytes=20 << 20),
        cost_estimate=pl.CostEstimate(
            flops=2 * count * TILES * NAUX * NAUX * 256, bytes_accessed=(8 + 2 * count) << 20, transcendentals=0
        ),
        name=name,
    )(tiles, *mine, *other, after)


def tile_kernel(
    tile_ref, occ_ref, rows_h, owners_h, blocks_h, sizes_h,
    m0, m1, m3, s0, s1, s3, m2a, m2b, s2a, s2b, c0, c1, c3, after, pay_ref,
    adj, vir, ct, g_ref, oexp, vexp, vacc, oacc, pay, occ_sum,
    rows, owners, blocks, sizes, sem, ct_sem, s_sem,
):
    t = pl.program_id(0)
    y = lax.axis_index("y")
    c = lax.axis_index("c")
    slots = chunk_slots(y)
    width = 256
    chunks = NAUX // width

    def scalars():
        pairs = ((rows_h, rows), (owners_h, owners), (blocks_h, blocks), (sizes_h, sizes))
        return [pltpu.make_async_copy(src, dst, s_sem.at[n]) for n, (src, dst) in enumerate(pairs)]

    def gathered():
        found = []

        def add(src, dst):
            found.append(pltpu.make_async_copy(src, dst, sem.at[len(found)]))

        for half, group, last in ((c, (m0, m1, m3), (m2a, m2b)), (1 - c, (s0, s1, s3), (s2a, s2b))):
            for src, at in zip(group, slots):
                add(src.at[:, :, pl.ds(512, 128)], vir.at[:, at, :, half_lanes(half, 128)])
            for n, src in enumerate(last):
                part = pl.ds(n * (NZ // 2), NZ // 2)
                add(src.at[:, :, pl.ds(512, 128)], vir.at[part, slots[3], :, half_lanes(half, 128)])
                add(src.at[:, :, pl.ds(0, 512)], adj.at[part, :, half_lanes(half, 512)])
        return found

    def contracted(tile):
        b = lax.rem(tile, 2)
        return [
            pltpu.make_async_copy(src.at[tile], ct.at[b, :, at], ct_sem.at[b, n])
            for n, (src, at) in enumerate(zip((c0, c1, c3), slots))
        ]

    @pl.when(t == 0)
    def _():
        for copy in scalars() + gathered() + contracted(0):
            copy.start()
        pay[...] = jnp.zeros_like(pay)
        pay[:, :, NAUX:] = jnp.full((BLOCKS, 8, 128), -1.0, F32)
        occ_sum[...] = jnp.zeros_like(occ_sum)
        for copy in scalars() + gathered():
            copy.wait()

    @pl.when(t + 1 < TILES)
    def _():
        for copy in contracted(t + 1):
            copy.start()

    @pl.when(t < TILES)
    def _():
        for copy in contracted(t):
            copy.wait()

    def reduce(n):
        lanes = slice(n * width, (n + 1) * width)
        vx = vexp[:, lanes]
        acc = jnp.zeros((BS, width), F32)
        for l in range(BS):
            g = g_ref[n % 2, l * BS : (l + 1) * BS, :]
            acc = acc + oexp[l : l + 1, lanes] * g
            oacc[l : l + 1, lanes] = jnp.sum(vx * g, axis=0, keepdims=True)
        vacc[:, lanes] = acc

    def flat(x):
        x = jnp.concatenate([x] * 4, axis=0).T[:BS]
        x = jnp.concatenate([x] * 8, axis=1)
        x = jnp.where(iota((BS, NAUX), 0) == iota((BS, NAUX), 1) // BS, x, 0.0)
        return jnp.sum(x, axis=0, keepdims=True)

    def collect(tile, valid):
        va = vacc[...]
        virt = va[:, :128]
        for m in range(1, 8):
            virt = virt + va[:, m * 128 : (m + 1) * 128]
        virt = virt + pltpu.roll(virt, 64, 1)
        virt = virt + pltpu.roll(virt, 32, 1)
        oa = oacc[...]
        high = oa.astype(BF16)
        rest = oa - high.astype(F32)
        mid = rest.astype(BF16)
        low = (rest - mid.astype(F32)).astype(BF16)
        group = (iota((NAUX, 128), 0) // BS == iota((NAUX, 128), 1) % BS).astype(BF16)
        occt = dot(high, group, 1, 0) + dot(mid, group, 1, 0) + dot(low, group, 1, 0)
        block = blocks[tile]
        dest = iota((BLOCKS, NAUX), 0)
        occ_sum[...] += jnp.where((dest == rows[tile]) & valid, flat(occt), 0.0)
        mine = jnp.where(dest == block, flat(virt), 0.0)
        label = jnp.where(iota((BLOCKS, 128), 0) == block, owners[tile].astype(F32), -1.0)
        whole = jnp.concatenate([mine, label], axis=1)
        pay[...] = jnp.where((iota((BLOCKS, 8, PAY), 1) == tile) & valid, whole[:, None, :], pay[...])

    @pl.when(t < TILES)
    def _():
        reduce(chunks - 1)
        b = lax.rem(t, 2)
        a = adj[...].reshape(256, NAUX)
        for n in range(chunks):
            lanes = slice(n * width, (n + 1) * width)
            ct[b, :, slots[3], :, lanes] = dot(a, tile_ref[t, lanes, :], 1, 1).astype(BF16).reshape(NZ, 32, width)
        def gram(n):
            lanes = slice(n * width, (n + 1) * width)
            g_ref[n % 2] = dot(tile_ref[t], ct[b, :, :, :, lanes].reshape(NAUX, width), 1, 0)

        collect(jnp.maximum(t - 1, 0), t > 0)
        gram(0)
        r = rows[t]
        occ_row = pick_row(occ_ref[...], r) * pair_mask(sizes[r])
        occ_sel = jnp.where(iota((BS, NAUX), 0) == iota((BS, NAUX), 1) % BS, occ_row, 0.0).astype(BF16)
        same = (iota((128, 128), 0) // BS == iota((128, 128), 1) // BS).astype(BF16)
        for m in range(8):
            lanes = slice(128 * m, 128 * (m + 1))
            oexp[:, lanes] = dot(occ_sel[:, lanes], same, 1, 0)
        col = owners[t] * BLOCKS + blocks[t]
        v32 = vir[col // 32, lax.rem(col // 8, NY)]
        pick = (iota((BS, BS), 1) == lax.rem(col, 8) * 4 + iota((BS, BS), 0) // 8).astype(BF16)
        spread = dot(pick, v32, 1, 0)
        spread = jnp.where(iota((BS, 256), 1) // BS == iota((BS, 256), 0) % 8, spread, 0.0).astype(BF16)
        fold = (iota((256, BS), 0) % BS == iota((256, BS), 1)).astype(BF16)
        v_block = dot(spread, fold, 1, 0).astype(BF16)
        repeat = (iota((BS, NAUX), 0) == iota((BS, NAUX), 1) % BS).astype(BF16)
        vexp[...] = dot(v_block, repeat, 0, 0)
        for n in range(1, chunks):
            gram(n)
            reduce(n - 1)

    @pl.when(t == TILES)
    def _():
        reduce(chunks - 1)
        collect(TILES - 1, True)
        total = occ_sum[...]
        top = total.astype(BF16).astype(F32)
        pay[:, 4:5, :NAUX] = top[:, None, :]
        pay[:, 5:6, :NAUX] = (total - top)[:, None, :]
        pay_ref[...] = pay[...].astype(BF16)


def form(tiles, occ_density, tile_rows, col_owner, col_block, block_sizes, gathered):
    return pl.pallas_call(
        tile_kernel,
        grid=(TILES + 1,),
        in_specs=[
            VMEM,
            pl.BlockSpec((BLOCKS, NAUX), lambda t: (0, 0), pipeline_mode=pl.Buffered(1)),
        ] + [ANY] * 18,
        out_specs=pl.BlockSpec((BLOCKS, 8, PAY), lambda t: (0, 0, 0)),
        scratch_shapes=[
            pltpu.VMEM((NZ, 32, NAUX), BF16),
            pltpu.VMEM((NZ, NY, 32, 256), BF16),
            pltpu.VMEM((2, NZ, NY, 32, NAUX), BF16),
            pltpu.VMEM((2, NAUX, 256), F32),
            pltpu.VMEM((BS, NAUX), F32),
            pltpu.VMEM((BS, NAUX), F32),
            pltpu.VMEM((BS, NAUX), F32),
            pltpu.VMEM((BS, NAUX), F32),
            pltpu.VMEM((BLOCKS, 8, PAY), F32),
            pltpu.VMEM((BLOCKS, NAUX), F32),
            pltpu.SMEM((TILES,), jnp.int32),
            pltpu.SMEM((TILES,), jnp.int32),
            pltpu.SMEM((TILES,), jnp.int32),
            pltpu.SMEM((BLOCKS,), jnp.int32),
            pltpu.SemaphoreType.DMA((14,)),
            pltpu.SemaphoreType.DMA((2, 3)),
            pltpu.SemaphoreType.DMA((4,)),
        ],
        out_shape=jax.ShapeDtypeStruct((BLOCKS, 8, PAY), BF16),
        compiler_params=pltpu.CompilerParams(vmem_limit_bytes=24 << 20),
        cost_estimate=pl.CostEstimate(flops=11 << 30, bytes_accessed=16 << 20, transcendentals=0),
        name="tiles",
    )(
        tiles,
        *map(in_hbm, (occ_density, tile_rows, col_owner.reshape(TILES), col_block, block_sizes)),
        *gathered,
    )


def route_kernel(sizes, got_ref, occ_ref, out_ref, spread):
    aux = lax.axis_index("x") * NC + lax.axis_index("c")
    got = got_ref[...].astype(F32)
    occ = jnp.sum(got[:, 4, :NAUX] + got[:, 5, :NAUX], axis=0, keepdims=True)
    occ_ref[...] = occ * pair_mask(sizes[aux]) * NORM
    flat = got.reshape(8 * BLOCKS, PAY)
    hot = (flat[:, NAUX:] == iota((8 * BLOCKS, 128), 1).astype(F32)).astype(BF16)
    terms = dot(hot, flat[:, :NAUX].astype(BF16), 0, 0)[: NZ * NY]
    for s in range(8):
        spread[:, s, :] = terms[:, 128 * s : 128 * (s + 1)]
    out_ref[...] = spread[...].astype(BF16)


def finish_kernel(sizes, got_ref, out_ref):
    aux = lax.axis_index("x") * NC + lax.axis_index("c")
    total = jnp.sum(got_ref[...].astype(F32), axis=0)
    row = jnp.concatenate([total[s : s + 1] for s in range(8)], axis=1)
    out_ref[...] = row * pair_mask(sizes[aux]) * NORM


def shards(adjoint, three_centre, occ_density, vir_density, block_sizes, tile_rows, col_owner, col_block):
    tiles = in_vmem(three_centre.reshape(TILES, BS * BS, NAUX))
    share = pl.pallas_call(
        prepare_kernel,
        out_shape=jax.ShapeDtypeStruct((NZ * NX, NC, 4, HALF), BF16),
        in_specs=[SMEM, VMEM, VMEM],
        out_specs=VMEM,
        name="prepare",
    )(block_sizes, adjoint, vir_density)
    share = share.reshape(NZ * NX * NC, 4, HALF)
    own = lax.all_to_all(share, ("z", "x", "c"), 0, 0, tiled=True).reshape(NZ, 32, HALF)
    ahead = [(i, (i + 1) % NY) for i in range(NY)]
    behind = [(i, (i - 1) % NY) for i in range(NY)]

    def sibling(x):
        return lax.ppermute(x, "c", [(0, 1), (1, 0)])

    def shift(x, pairs):
        return lax.ppermute(x, "y", pairs)

    m1 = shift(own, ahead)
    m3 = shift(own, behind)
    s0 = sibling(own)
    c0, token = contract(tiles, [own], [s0], own, "contract_own")
    m1, m3, token = lax.optimization_barrier((m1, m3, token))
    m2a = shift(m1[: NZ // 2], ahead)
    m2b = shift(m3[NZ // 2 :], behind)
    s1 = sibling(m1)
    s3 = sibling(m3)
    c1, c3, token = contract(tiles, [m1, m3], [s1, s3], token, "contract_sides")
    m2a, m2b, token = lax.optimization_barrier((m2a, m2b, token))
    s2a = sibling(m2a)
    s2b = sibling(m2b)

    pay = form(
        tiles, occ_density, tile_rows, col_owner, col_block, block_sizes,
        (own, m1, m3, s0, s1, s3, m2a, m2b, s2a, s2b, c0, c1, c3, token),
    )
    got = lax.all_to_all(pay, ("x", "c"), 0, 0, tiled=True)
    occ_grad, terms = pl.pallas_call(
        route_kernel,
        out_shape=(
            jax.ShapeDtypeStruct((1, NAUX), F32),
            jax.ShapeDtypeStruct((NZ * NY, 8, 128), BF16),
        ),
        in_specs=[SMEM, VMEM],
        out_specs=(VMEM, VMEM),
        scratch_shapes=[pltpu.VMEM((NZ * NY, 8, 128), F32)],
        name="route",
    )(block_sizes, got)
    back = lax.all_to_all(terms, ("z", "y"), 0, 0, tiled=True)
    vir_grad = pl.pallas_call(
        finish_kernel,
        out_shape=jax.ShapeDtypeStruct((1, NAUX), F32),
        in_specs=[SMEM, VMEM],
        out_specs=VMEM,
        name="finish",
    )(block_sizes, back)
    return occ_grad, vir_grad


def solution(mesh):
    grid = Mesh(mesh.devices.reshape(NZ, NY, NX, NC), ("z", "y", "x", "c"))
    every = ("z", "y", "x", "c")
    blk = ("z", "y")
    in_specs = (
        P(every, None),
        P(every, None, None, None),
        P(blk, None),
        P(blk, None),
        P(blk),
        P(every),
        P(every, None),
        P(every),
    )
    out_specs = (P(every, None), P(every, None))
    return jax.shard_map(shards, mesh=grid, in_specs=in_specs, out_specs=out_specs, check_vma=False)
```

```python
import functools
import jax
import jax.numpy as jnp
from jax import lax
from jax.experimental import pallas as pl
from jax.experimental.pallas import tpu as pltpu
from jax.sharding import Mesh, PartitionSpec as P

BS = 32
NAUX = 1024
HALF = 640
NZ, NY, NX, NC = 8, 4, 4, 2
TILES = 4
BLOCKS = 8
F32 = jnp.float32
BF16 = jnp.bfloat16
NORM = NAUX ** -0.5
PAY = NAUX + 128
ANY = pl.BlockSpec(memory_space=pl.ANY)
SMEM = pl.BlockSpec(memory_space=pltpu.SMEM)
VMEM = pl.BlockSpec(memory_space=pltpu.VMEM)


def dot(a, b, ca, cb):
    return lax.dot_general(a, b, (((ca,), (cb,)), ((), ())), preferred_element_type=F32)


def iota(shape, dim):
    return lax.broadcasted_iota(jnp.int32, shape, dim)


def pair_mask(size):
    lane = iota((1, NAUX), 1)
    return ((lane // BS < size) & (lane % BS < size)).astype(F32)


def pick_row(block, row):
    return jnp.sum(jnp.where(iota(block.shape, 0) == row, block.astype(F32), 0.0), axis=0, keepdims=True)


def prepare_kernel(sizes_ref, adj_ref, vir_ref, out_ref, mask_ref):
    aux = lax.axis_index("x") * NC + lax.axis_index("c")
    size = jnp.sum(jnp.where(iota((1, BLOCKS), 1) == aux, sizes_ref[...], 0), axis=1, keepdims=True)
    mask = pair_mask(size)
    mask_ref[...] = mask * NORM
    row = (pick_row(vir_ref[...], aux) * mask).astype(BF16)
    quarters = jnp.concatenate([row[:, 256 * r : 256 * (r + 1)] for r in range(4)], axis=0)
    for c in range(NC):
        share = jnp.concatenate(
            [adj_ref[:, 512 * c : 512 * (c + 1)], quarters[:, 128 * c : 128 * (c + 1)]], axis=1
        )
        out_ref[:, c] = jnp.broadcast_to(share[None], (NZ * NX, 4, HALF))


def chunk_slots(y):
    return [lax.rem(y + NY - shift, NY) for shift in (0, 1, 3, 2)]


def half_lanes(half, width):
    return pl.ds(pl.multiple_of(half * width, width), width)


def contract_kernel(count, tile_ref, *refs):
    mine, other = refs[:count], refs[count : 2 * count]
    outs = refs[2 * count + 1 : 3 * count + 1]
    token, adj, sem = refs[3 * count + 1 :]
    c = lax.axis_index("c")

    def copies():
        found = []
        for half, group in ((c, mine), (1 - c, other)):
            for m, src in enumerate(group):
                found.append(pltpu.make_async_copy(
                    src.at[:, :, pl.ds(0, 512)], adj.at[m, :, :, half_lanes(half, 512)], sem.at[len(found)]))
        return found

    @pl.when(pl.program_id(0) == 0)
    def _():
        for copy in copies():
            copy.start()
        token[...] = jnp.zeros_like(token)
        for copy in copies():
            copy.wait()

    t = pl.program_id(0)
    for m in range(count):
        a = adj[m].reshape(256, NAUX)
        for n in range(4):
            lanes = slice(256 * n, 256 * (n + 1))
            outs[m][0, :, :, lanes] = dot(a, tile_ref[t, lanes, :], 1, 1).astype(BF16).reshape(NZ, 32, 256)


def in_hbm(x):
    return pltpu.with_memory_space_constraint(x, pltpu.HBM)


def in_vmem(x):
    return pltpu.with_memory_space_constraint(x, pltpu.VMEM)


def contract(tiles, mine, other, after, name):
    count = len(mine)
    return pl.pallas_call(
        functools.partial(contract_kernel, count),
        grid=(TILES,),
        in_specs=[VMEM] + [ANY] * (2 * count + 1),
        out_specs=[pl.BlockSpec((1, NZ, 32, NAUX), lambda t: (t, 0, 0, 0))] * count
        + [pl.BlockSpec((8, 128), lambda t: (0, 0))],
        out_shape=[jax.ShapeDtypeStruct((TILES, NZ, 32, NAUX), BF16)] * count
        + [jax.ShapeDtypeStruct((8, 128), F32)],
        scratch_shapes=[
            pltpu.VMEM((count, NZ, 32, NAUX), BF16),
            pltpu.SemaphoreType.DMA((2 * count,)),
        ],
        compiler_params=pltpu.CompilerParams(vmem_limit_bytes=20 << 20),
        cost_estimate=pl.CostEstimate(
            flops=2 * count * TILES * NAUX * NAUX * 256, bytes_accessed=(8 + 2 * count) << 20, transcendentals=0
        ),
        name=name,
    )(tiles, *mine, *other, after)


def expand_kernel(rows, owners, blocks, sizes, occ_ref, oexp_ref, meta_ref, first_ref):
    same = (iota((128, 128), 0) // BS == iota((128, 128), 1) // BS).astype(BF16)
    for t in range(TILES):
        r = rows[t]
        occ_row = pick_row(occ_ref[...], r) * pair_mask(sizes[r])
        occ_sel = jnp.where(iota((BS, NAUX), 0) == iota((BS, NAUX), 1) % BS, occ_row, 0.0).astype(BF16)
        for m in range(8):
            lanes = slice(128 * m, 128 * (m + 1))
            oexp_ref[t, :, lanes] = dot(occ_sel[:, lanes], same, 1, 0)
        for n, value in enumerate((r, blocks[t], owners[t])):
            meta_ref[t, n] = jnp.full((8, 128), value, jnp.int32)
        col = owners[t] * BLOCKS + blocks[t]
        first_ref[t * BS : (t + 1) * BS, :] = 4 * col + iota((BS, 128), 0) // 8


def expand(tile_rows, col_owner, col_block, block_sizes, occ_density):
    return pl.pallas_call(
        expand_kernel,
        in_specs=[SMEM] * 4 + [VMEM],
        out_specs=[VMEM] * 3,
        out_shape=[
            jax.ShapeDtypeStruct((TILES, BS, NAUX), F32),
            jax.ShapeDtypeStruct((TILES, 3, 8, 128), jnp.int32),
            jax.ShapeDtypeStruct((TILES * BS, 128), jnp.int32),
        ],
        name="expand",
    )(tile_rows, col_owner.reshape(TILES), col_block, block_sizes, occ_density)


def tile_kernel(
    tile_ref, oexp, meta_ref, first_ref,
    m0, m1, m3, s0, s1, s3, m2a, m2b, s2a, s2b, c0, c1, c3, after, pay_ref,
    adj, vir, ct, g_ref, vexp, vacc, oacc, pay, occ_sum, sem, ct_sem,
):
    t = pl.program_id(0)
    y = lax.axis_index("y")
    c = lax.axis_index("c")
    slots = chunk_slots(y)
    width = 256
    chunks = NAUX // width

    def gathered():
        found = []

        def add(src, dst):
            found.append(pltpu.make_async_copy(src, dst, sem.at[len(found)]))

        for half, group, last in ((c, (m0, m1, m3), (m2a, m2b)), (1 - c, (s0, s1, s3), (s2a, s2b))):
            for src, at in zip(group, slots):
                add(src.at[:, :, pl.ds(512, 128)], vir.at[:, at, :, half_lanes(half, 128)])
            for n, src in enumerate(last):
                part = pl.ds(n * (NZ // 2), NZ // 2)
                add(src.at[:, :, pl.ds(512, 128)], vir.at[part, slots[3], :, half_lanes(half, 128)])
                add(src.at[:, :, pl.ds(0, 512)], adj.at[part, :, half_lanes(half, 512)])
        return found

    def contracted(tile):
        b = lax.rem(tile, 2)
        return [
            pltpu.make_async_copy(src.at[tile], ct.at[b, :, at], ct_sem.at[b, n])
            for n, (src, at) in enumerate(zip((c0, c1, c3), slots))
        ]

    @pl.when(t == 0)
    def _():
        for copy in gathered() + contracted(0):
            copy.start()
        pay[...] = jnp.zeros_like(pay)
        pay[:, :, NAUX:] = jnp.full((BLOCKS, 8, 128), -1.0, F32)
        occ_sum[...] = jnp.zeros_like(occ_sum)
        for copy in gathered():
            copy.wait()
        pick = jnp.concatenate(
            [first_ref[...] == iota((TILES * BS, 128), 1) + 128 * m for m in range(8)], axis=1
        ).astype(BF16)
        spread = dot(pick, vir[...].reshape(NAUX, 256), 1, 0)
        group = iota((TILES * BS, 256), 1) // BS == iota((TILES * BS, 256), 0) % 8
        spread = jnp.where(group, spread, 0.0).astype(BF16)
        fold = (iota((256, BS), 0) % BS == iota((256, BS), 1)).astype(BF16)
        v_blocks = dot(spread, fold, 1, 0).astype(BF16)
        repeat = (iota((BS, NAUX), 0) == iota((BS, NAUX), 1) % BS).astype(BF16)
        for tile in range(TILES):
            vexp[tile] = dot(v_blocks[tile * BS : (tile + 1) * BS], repeat, 0, 0)

    @pl.when(t + 1 < TILES)
    def _():
        for copy in contracted(t + 1):
            copy.start()

    @pl.when(t < TILES)
    def _():
        for copy in contracted(t):
            copy.wait()

    def reduce(n, tile):
        lanes = slice(n * width, (n + 1) * width)
        vx = vexp[tile, :, lanes]
        acc = jnp.zeros((BS, width), F32)
        for l in range(BS):
            g = g_ref[n % 2, l * BS : (l + 1) * BS, :]
            acc = acc + oexp[tile, l : l + 1, lanes] * g
            oacc[l : l + 1, lanes] = jnp.sum(vx * g, axis=0, keepdims=True)
        vacc[:, lanes] = acc

    def flat(x):
        x = jnp.concatenate([x] * 4, axis=0).T[:BS]
        x = jnp.concatenate([x] * 8, axis=1)
        x = jnp.where(iota((BS, NAUX), 0) == iota((BS, NAUX), 1) // BS, x, 0.0)
        return jnp.sum(x, axis=0, keepdims=True)

    def collect(tile, valid):
        va = vacc[...]
        virt = va[:, :128]
        for m in range(1, 8):
            virt = virt + va[:, m * 128 : (m + 1) * 128]
        virt = virt + pltpu.roll(virt, 64, 1)
        virt = virt + pltpu.roll(virt, 32, 1)
        oa = oacc[...]
        high = oa.astype(BF16)
        rest = oa - high.astype(F32)
        mid = rest.astype(BF16)
        low = (rest - mid.astype(F32)).astype(BF16)
        group = (iota((NAUX, 128), 0) // BS == iota((NAUX, 128), 1) % BS).astype(BF16)
        occt = dot(high, group, 1, 0) + dot(mid, group, 1, 0) + dot(low, group, 1, 0)
        dest = iota((BLOCKS, 128), 0)
        row_here = jnp.concatenate([dest == meta_ref[tile, 0]] * 8, axis=1)
        block_here = dest == meta_ref[tile, 1]
        occ_sum[...] += jnp.where(row_here & valid, flat(occt), 0.0)
        mine = jnp.where(jnp.concatenate([block_here] * 8, axis=1), flat(virt), 0.0)
        label = jnp.where(block_here, meta_ref[tile, 2].astype(F32), -1.0)
        whole = jnp.concatenate([mine, label], axis=1)
        pay[...] = jnp.where((iota((BLOCKS, 8, PAY), 1) == tile) & valid, whole[:, None, :], pay[...])

    @pl.when(t < TILES)
    def _():
        reduce(chunks - 1, jnp.maximum(t - 1, 0))
        b = lax.rem(t, 2)
        a = adj[...].reshape(256, NAUX)
        for n in range(chunks):
            lanes = slice(n * width, (n + 1) * width)
            ct[b, :, slots[3], :, lanes] = dot(a, tile_ref[t, lanes, :], 1, 1).astype(BF16).reshape(NZ, 32, width)
        def gram(n):
            lanes = slice(n * width, (n + 1) * width)
            g_ref[n % 2] = dot(tile_ref[t], ct[b, :, :, :, lanes].reshape(NAUX, width), 1, 0)

        collect(jnp.maximum(t - 1, 0), t > 0)
        gram(0)
        for n in range(1, chunks):
            gram(n)
            reduce(n - 1, t)

    @pl.when(t == TILES)
    def _():
        reduce(chunks - 1, TILES - 1)
        collect(TILES - 1, True)
        total = occ_sum[...]
        top = total.astype(BF16).astype(F32)
        pay[:, 4:5, :NAUX] = top[:, None, :]
        pay[:, 5:6, :NAUX] = (total - top)[:, None, :]
        pay_ref[...] = pay[...].astype(BF16)


def form(tiles, oexp, meta, first, gathered):
    return pl.pallas_call(
        tile_kernel,
        grid=(TILES + 1,),
        in_specs=[VMEM] * 4 + [ANY] * 14,
        out_specs=pl.BlockSpec((BLOCKS, 8, PAY), lambda t: (0, 0, 0)),
        scratch_shapes=[
            pltpu.VMEM((NZ, 32, NAUX), BF16),
            pltpu.VMEM((NZ, NY, 32, 256), BF16),
            pltpu.VMEM((2, NZ, NY, 32, NAUX), BF16),
            pltpu.VMEM((2, NAUX, 256), F32),
            pltpu.VMEM((TILES, BS, NAUX), F32),
            pltpu.VMEM((BS, NAUX), F32),
            pltpu.VMEM((BS, NAUX), F32),
            pltpu.VMEM((BLOCKS, 8, PAY), F32),
            pltpu.VMEM((BLOCKS, NAUX), F32),
            pltpu.SemaphoreType.DMA((14,)),
            pltpu.SemaphoreType.DMA((2, 3)),
        ],
        out_shape=jax.ShapeDtypeStruct((BLOCKS, 8, PAY), BF16),
        compiler_params=pltpu.CompilerParams(vmem_limit_bytes=24 << 20),
        cost_estimate=pl.CostEstimate(flops=11 << 30, bytes_accessed=16 << 20, transcendentals=0),
        name="tiles",
    )(tiles, oexp, meta, first, *gathered)


def route_kernel(mask_ref, got_ref, occ_ref, out_ref, spread):
    got = got_ref[...].astype(F32)
    occ = jnp.sum(got[:, 4, :NAUX] + got[:, 5, :NAUX], axis=0, keepdims=True)
    occ_ref[...] = occ * mask_ref[...]
    flat = got.reshape(8 * BLOCKS, PAY)
    hot = (flat[:, NAUX:] == iota((8 * BLOCKS, 128), 1).astype(F32)).astype(BF16)
    terms = dot(hot, flat[:, :NAUX].astype(BF16), 0, 0)[: NZ * NY]
    for s in range(8):
        spread[:, s, :] = terms[:, 128 * s : 128 * (s + 1)]
    out_ref[...] = spread[...].astype(BF16)


def finish_kernel(mask_ref, got_ref, out_ref):
    total = jnp.sum(got_ref[...].astype(F32), axis=0)
    row = jnp.concatenate([total[s : s + 1] for s in range(8)], axis=1)
    out_ref[...] = row * mask_ref[...]


def shards(adjoint, three_centre, occ_density, vir_density, block_sizes, tile_rows, col_owner, col_block):
    tiles = in_vmem(three_centre.reshape(TILES, BS * BS, NAUX))
    share, mask = pl.pallas_call(
        prepare_kernel,
        out_shape=(
            jax.ShapeDtypeStruct((NZ * NX, NC, 4, HALF), BF16),
            jax.ShapeDtypeStruct((1, NAUX), F32),
        ),
        in_specs=[VMEM] * 3,
        out_specs=(VMEM, VMEM),
        name="prepare",
    )(block_sizes.reshape(1, BLOCKS), adjoint, vir_density)
    share = share.reshape(NZ * NX * NC, 4, HALF)
    own = lax.all_to_all(share, ("z", "x", "c"), 0, 0, tiled=True).reshape(NZ, 32, HALF)
    ahead = [(i, (i + 1) % NY) for i in range(NY)]
    behind = [(i, (i - 1) % NY) for i in range(NY)]

    def sibling(x):
        return lax.ppermute(x, "c", [(0, 1), (1, 0)])

    def shift(x, pairs):
        return lax.ppermute(x, "y", pairs)

    m1 = shift(own, ahead)
    m3 = shift(own, behind)
    s0 = sibling(own)
    oexp, meta, first = expand(tile_rows, col_owner, col_block, block_sizes, occ_density)
    s0, oexp, meta, first = lax.optimization_barrier((s0, oexp, meta, first))
    c0, token = contract(tiles, [own], [s0], own, "contract_own")
    m1, m3, token = lax.optimization_barrier((m1, m3, token))
    m2a = shift(m1[: NZ // 2], ahead)
    m2b = shift(m3[NZ // 2 :], behind)
    s1 = sibling(m1)
    s3 = sibling(m3)
    c1, c3, token = contract(tiles, [m1, m3], [s1, s3], token, "contract_sides")
    m2a, m2b, token = lax.optimization_barrier((m2a, m2b, token))
    s2a = sibling(m2a)
    s2b = sibling(m2b)

    pay = form(
        tiles, oexp, meta, first,
        (own, m1, m3, s0, s1, s3, m2a, m2b, s2a, s2b, c0, c1, c3, token),
    )
    got = lax.all_to_all(pay, ("x", "c"), 0, 0, tiled=True)
    occ_grad, terms = pl.pallas_call(
        route_kernel,
        out_shape=(
            jax.ShapeDtypeStruct((1, NAUX), F32),
            jax.ShapeDtypeStruct((NZ * NY, 8, 128), BF16),
        ),
        in_specs=[VMEM, VMEM],
        out_specs=(VMEM, VMEM),
        scratch_shapes=[pltpu.VMEM((NZ * NY, 8, 128), F32)],
        name="route",
    )(mask, got)
    back = lax.all_to_all(terms, ("z", "y"), 0, 0, tiled=True)
    vir_grad = pl.pallas_call(
        finish_kernel,
        out_shape=jax.ShapeDtypeStruct((1, NAUX), F32),
        in_specs=[VMEM, VMEM],
        out_specs=VMEM,
        name="finish",
    )(mask, back)
    return occ_grad, vir_grad


def solution(mesh):
    grid = Mesh(mesh.devices.reshape(NZ, NY, NX, NC), ("z", "y", "x", "c"))
    every = ("z", "y", "x", "c")
    blk = ("z", "y")
    in_specs = (
        P(every, None),
        P(every, None, None, None),
        P(blk, None),
        P(blk, None),
        P(blk),
        P(every),
        P(every, None),
        P(every),
    )
    out_specs = (P(every, None), P(every, None))
    return jax.shard_map(shards, mesh=grid, in_specs=in_specs, out_specs=out_specs, check_vma=False)
```

```python
import functools
import jax
import jax.numpy as jnp
from jax import lax
from jax.experimental import pallas as pl
from jax.experimental.pallas import tpu as pltpu
from jax.sharding import Mesh, PartitionSpec as P

BS = 32
NAUX = 1024
HALF = 640
NZ, NY, NX, NC = 8, 4, 4, 2
TILES = 4
BLOCKS = 8
F32 = jnp.float32
BF16 = jnp.bfloat16
NORM = NAUX ** -0.5
PAY = NAUX + 128
ANY = pl.BlockSpec(memory_space=pl.ANY)
SMEM = pl.BlockSpec(memory_space=pltpu.SMEM)
VMEM = pl.BlockSpec(memory_space=pltpu.VMEM)


def dot(a, b, ca, cb):
    return lax.dot_general(a, b, (((ca,), (cb,)), ((), ())), preferred_element_type=F32)


def iota(shape, dim):
    return lax.broadcasted_iota(jnp.int32, shape, dim)


def pair_mask(size):
    return live_mask(iota((1, NAUX), 1), size)


def live_mask(pair, size):
    return ((pair // BS < size) & (pair % BS < size)).astype(F32)


def pick_row(block, row):
    return jnp.sum(jnp.where(iota(block.shape, 0) == row, block.astype(F32), 0.0), axis=0, keepdims=True)


def prepare_kernel(sizes_ref, adj_ref, vir_ref, out_ref, mask_ref, square_ref):
    aux = lax.axis_index("x") * NC + lax.axis_index("c")
    size = jnp.sum(jnp.where(iota((1, BLOCKS), 1) == aux, sizes_ref[...], 0), axis=1, keepdims=True)
    mask = pair_mask(size)
    mask_ref[...] = mask * NORM
    square_ref[...] = live_mask(iota((8, 128), 0) * 128 + iota((8, 128), 1), size) * NORM
    row = (pick_row(vir_ref[...], aux) * mask).astype(BF16)
    quarters = jnp.concatenate([row[:, 256 * r : 256 * (r + 1)] for r in range(4)], axis=0)
    for c in range(NC):
        share = jnp.concatenate(
            [adj_ref[:, 512 * c : 512 * (c + 1)], quarters[:, 128 * c : 128 * (c + 1)]], axis=1
        )
        out_ref[:, c] = jnp.broadcast_to(share[None], (NZ * NX, 4, HALF))


def row_sums(parts):
    row = iota(parts[0].shape, 0)
    for step in (1, 2, 4):
        first = row // step % 2 == 0
        parts = [
            jnp.where(first, a, b) + pltpu.roll(jnp.where(first, b, a), step, 0)
            for a, b in zip(parts[::2], parts[1::2])
        ]
    return parts[0]


def chunk_slots(y):
    return [lax.rem(y + NY - shift, NY) for shift in (0, 1, 3, 2)]


def half_lanes(half, width):
    return pl.ds(pl.multiple_of(half * width, width), width)


def contract_kernel(count, tile_ref, *refs):
    mine, other = refs[:count], refs[count : 2 * count]
    outs = refs[2 * count + 1 : 3 * count + 1]
    token, adj, sem = refs[3 * count + 1 :]
    c = lax.axis_index("c")

    def copies():
        found = []
        for half, group in ((c, mine), (1 - c, other)):
            for m, src in enumerate(group):
                found.append(pltpu.make_async_copy(
                    src.at[:, :, pl.ds(0, 512)], adj.at[m, :, :, half_lanes(half, 512)], sem.at[len(found)]))
        return found

    @pl.when(pl.program_id(0) == 0)
    def _():
        for copy in copies():
            copy.start()
        token[...] = jnp.zeros_like(token)
        for copy in copies():
            copy.wait()

    t = pl.program_id(0)
    for m in range(count):
        a = adj[m].reshape(256, NAUX)
        for n in range(4):
            lanes = slice(256 * n, 256 * (n + 1))
            outs[m][0, :, :, lanes] = dot(a, tile_ref[t, lanes, :], 1, 1).astype(BF16).reshape(NZ, 32, 256)


def in_hbm(x):
    return pltpu.with_memory_space_constraint(x, pltpu.HBM)


def in_vmem(x):
    return pltpu.with_memory_space_constraint(x, pltpu.VMEM)


def contract(tiles, mine, other, after, name):
    count = len(mine)
    return pl.pallas_call(
        functools.partial(contract_kernel, count),
        grid=(TILES,),
        in_specs=[VMEM] + [ANY] * (2 * count + 1),
        out_specs=[pl.BlockSpec((1, NZ, 32, NAUX), lambda t: (t, 0, 0, 0))] * count
        + [pl.BlockSpec((8, 128), lambda t: (0, 0))],
        out_shape=[jax.ShapeDtypeStruct((TILES, NZ, 32, NAUX), BF16)] * count
        + [jax.ShapeDtypeStruct((8, 128), F32)],
        scratch_shapes=[
            pltpu.VMEM((count, NZ, 32, NAUX), BF16),
            pltpu.SemaphoreType.DMA((2 * count,)),
        ],
        compiler_params=pltpu.CompilerParams(vmem_limit_bytes=20 << 20),
        cost_estimate=pl.CostEstimate(
            flops=2 * count * TILES * NAUX * NAUX * 256, bytes_accessed=(8 + 2 * count) << 20, transcendentals=0
        ),
        name=name,
    )(tiles, *mine, *other, after)


def expand_kernel(rows, owners, blocks, sizes, occ_ref, oexp_ref, meta_ref, first_ref):
    same = (iota((128, 128), 0) // BS == iota((128, 128), 1) // BS).astype(BF16)
    for t in range(TILES):
        r = rows[t]
        occ_row = pick_row(occ_ref[...], r) * pair_mask(sizes[r])
        occ_sel = jnp.where(iota((BS, NAUX), 0) == iota((BS, NAUX), 1) % BS, occ_row, 0.0).astype(BF16)
        for m in range(8):
            lanes = slice(128 * m, 128 * (m + 1))
            oexp_ref[t, :, lanes] = dot(occ_sel[:, lanes], same, 1, 0)
        for n, value in enumerate((r, blocks[t], owners[t])):
            meta_ref[t, n] = jnp.full((8, 128), value, jnp.int32)
        col = owners[t] * BLOCKS + blocks[t]
        first_ref[t * BS : (t + 1) * BS, :] = 4 * col + iota((BS, 128), 0) // 8


def expand(tile_rows, col_owner, col_block, block_sizes, occ_density):
    return pl.pallas_call(
        expand_kernel,
        in_specs=[SMEM] * 4 + [VMEM],
        out_specs=[VMEM] * 3,
        out_shape=[
            jax.ShapeDtypeStruct((TILES, BS, NAUX), F32),
            jax.ShapeDtypeStruct((TILES, 3, 8, 128), jnp.int32),
            jax.ShapeDtypeStruct((TILES * BS, 128), jnp.int32),
        ],
        name="expand",
    )(tile_rows, col_owner.reshape(TILES), col_block, block_sizes, occ_density)


def tile_kernel(
    tile_ref, oexp, meta_ref, first_ref,
    m0, m1, m3, s0, s1, s3, m2a, m2b, s2a, s2b, c0, c1, c3, after, pay_ref,
    adj, vir, ct, g_ref, vexp, vacc, oacc, pay, occ_sum, sem, ct_sem,
):
    t = pl.program_id(0)
    y = lax.axis_index("y")
    c = lax.axis_index("c")
    slots = chunk_slots(y)
    width = 256
    chunks = NAUX // width

    def gathered():
        found = []

        def add(src, dst):
            found.append(pltpu.make_async_copy(src, dst, sem.at[len(found)]))

        for half, group, last in ((c, (m0, m1, m3), (m2a, m2b)), (1 - c, (s0, s1, s3), (s2a, s2b))):
            for src, at in zip(group, slots):
                add(src.at[:, :, pl.ds(512, 128)], vir.at[:, at, :, half_lanes(half, 128)])
            for n, src in enumerate(last):
                part = pl.ds(n * (NZ // 2), NZ // 2)
                add(src.at[:, :, pl.ds(512, 128)], vir.at[part, slots[3], :, half_lanes(half, 128)])
                add(src.at[:, :, pl.ds(0, 512)], adj.at[part, :, half_lanes(half, 512)])
        return found

    def contracted(tile):
        b = lax.rem(tile, 2)
        return [
            pltpu.make_async_copy(src.at[tile], ct.at[b, :, at], ct_sem.at[b, n])
            for n, (src, at) in enumerate(zip((c0, c1, c3), slots))
        ]

    @pl.when(t == 0)
    def _():
        for copy in gathered() + contracted(0):
            copy.start()
        pay[...] = jnp.zeros_like(pay)
        pay[:, :, NAUX:] = jnp.full((BLOCKS, 8, 128), -1.0, F32)
        occ_sum[...] = jnp.zeros_like(occ_sum)
        for copy in gathered():
            copy.wait()
        pick = jnp.concatenate(
            [first_ref[...] == iota((TILES * BS, 128), 1) + 128 * m for m in range(8)], axis=1
        ).astype(BF16)
        spread = dot(pick, vir[...].reshape(NAUX, 256), 1, 0)
        group = iota((TILES * BS, 256), 1) // BS == iota((TILES * BS, 256), 0) % 8
        spread = jnp.where(group, spread, 0.0).astype(BF16)
        fold = (iota((256, BS), 0) % BS == iota((256, BS), 1)).astype(BF16)
        v_blocks = dot(spread, fold, 1, 0).astype(BF16)
        repeat = (iota((BS, NAUX), 0) == iota((BS, NAUX), 1) % BS).astype(BF16)
        for tile in range(TILES):
            vexp[tile] = dot(v_blocks[tile * BS : (tile + 1) * BS], repeat, 0, 0)

    @pl.when(t + 1 < TILES)
    def _():
        for copy in contracted(t + 1):
            copy.start()

    @pl.when(t < TILES)
    def _():
        for copy in contracted(t):
            copy.wait()

    def reduce(n, tile):
        lanes = slice(n * width, (n + 1) * width)
        vx = vexp[tile, :, lanes]
        acc = jnp.zeros((BS, width), F32)
        for base in range(0, BS, 8):
            parts = []
            for l in range(base, base + 8):
                g = g_ref[n % 2, l * BS : (l + 1) * BS, :]
                acc = acc + oexp[tile, l : l + 1, lanes] * g
                p = vx * g
                parts.append((p[:8] + p[8:16]) + (p[16:24] + p[24:]))
            oacc[base : base + 8, lanes] = row_sums(parts)
        vacc[:, lanes] = acc

    def flat(x):
        x = jnp.concatenate([x] * 4, axis=0).T[:BS]
        x = jnp.concatenate([x] * 8, axis=1)
        x = jnp.where(iota((BS, NAUX), 0) == iota((BS, NAUX), 1) // BS, x, 0.0)
        return jnp.sum(x, axis=0, keepdims=True)

    def collect(tile, valid):
        va = vacc[...]
        virt = va[:, :128]
        for m in range(1, 8):
            virt = virt + va[:, m * 128 : (m + 1) * 128]
        virt = virt + pltpu.roll(virt, 64, 1)
        virt = virt + pltpu.roll(virt, 32, 1)
        oa = oacc[...]
        high = oa.astype(BF16)
        rest = oa - high.astype(F32)
        low = rest.astype(BF16)
        group = (iota((NAUX, 128), 0) // BS == iota((NAUX, 128), 1) % BS).astype(BF16)
        occt = dot(high, group, 1, 0) + dot(low, group, 1, 0)
        dest = iota((BLOCKS, 128), 0)
        row_here = jnp.concatenate([dest == meta_ref[tile, 0]] * 8, axis=1)
        block_here = dest == meta_ref[tile, 1]
        occ_sum[...] += jnp.where(row_here & valid, flat(occt), 0.0)
        mine = jnp.where(jnp.concatenate([block_here] * 8, axis=1), flat(virt), 0.0)
        label = jnp.where(block_here, meta_ref[tile, 2].astype(F32), -1.0)
        whole = jnp.concatenate([mine, label], axis=1)
        pay[...] = jnp.where((iota((BLOCKS, 8, PAY), 1) == tile) & valid, whole[:, None, :], pay[...])

    @pl.when(t < TILES)
    def _():
        reduce(chunks - 1, jnp.maximum(t - 1, 0))
        b = lax.rem(t, 2)
        a = adj[...].reshape(256, NAUX)
        for n in range(chunks):
            lanes = slice(n * width, (n + 1) * width)
            ct[b, :, slots[3], :, lanes] = dot(a, tile_ref[t, lanes, :], 1, 1).astype(BF16).reshape(NZ, 32, width)
        def gram(n):
            lanes = slice(n * width, (n + 1) * width)
            g_ref[n % 2] = dot(tile_ref[t], ct[b, :, :, :, lanes].reshape(NAUX, width), 1, 0)

        collect(jnp.maximum(t - 1, 0), t > 0)
        gram(0)
        for n in range(1, chunks):
            gram(n)
            reduce(n - 1, t)

    @pl.when(t == TILES)
    def _():
        reduce(chunks - 1, TILES - 1)
        collect(TILES - 1, True)
        total = occ_sum[...]
        top = total.astype(BF16).astype(F32)
        pay[:, 4:5, :NAUX] = top[:, None, :]
        pay[:, 5:6, :NAUX] = (total - top)[:, None, :]
        pay_ref[...] = pay[...].astype(BF16)


def form(tiles, oexp, meta, first, gathered):
    return pl.pallas_call(
        tile_kernel,
        grid=(TILES + 1,),
        in_specs=[VMEM] * 4 + [ANY] * 14,
        out_specs=pl.BlockSpec((BLOCKS, 8, PAY), lambda t: (0, 0, 0)),
        scratch_shapes=[
            pltpu.VMEM((NZ, 32, NAUX), BF16),
            pltpu.VMEM((NZ, NY, 32, 256), BF16),
            pltpu.VMEM((2, NZ, NY, 32, NAUX), BF16),
            pltpu.VMEM((2, NAUX, 256), F32),
            pltpu.VMEM((TILES, BS, NAUX), F32),
            pltpu.VMEM((BS, NAUX), F32),
            pltpu.VMEM((BS, NAUX), F32),
            pltpu.VMEM((BLOCKS, 8, PAY), F32),
            pltpu.VMEM((BLOCKS, NAUX), F32),
            pltpu.SemaphoreType.DMA((14,)),
            pltpu.SemaphoreType.DMA((2, 3)),
        ],
        out_shape=jax.ShapeDtypeStruct((BLOCKS, 8, PAY), BF16),
        compiler_params=pltpu.CompilerParams(vmem_limit_bytes=24 << 20),
        cost_estimate=pl.CostEstimate(flops=11 << 30, bytes_accessed=16 << 20, transcendentals=0),
        name="tiles",
    )(tiles, oexp, meta, first, *gathered)


def route_kernel(mask_ref, got_ref, occ_ref, out_ref, spread):
    got = got_ref[...].astype(F32)
    occ = jnp.sum(got[:, 4, :NAUX] + got[:, 5, :NAUX], axis=0, keepdims=True)
    occ_ref[...] = occ * mask_ref[...]
    flat = got.reshape(8 * BLOCKS, PAY)
    hot = (flat[:, NAUX:] == iota((8 * BLOCKS, 128), 1).astype(F32)).astype(BF16)
    terms = dot(hot, flat[:, :NAUX].astype(BF16), 0, 0)[: NZ * NY]
    for s in range(8):
        spread[:, s, :] = terms[:, 128 * s : 128 * (s + 1)]
    out_ref[...] = spread[...].astype(BF16)


def shards(adjoint, three_centre, occ_density, vir_density, block_sizes, tile_rows, col_owner, col_block):
    tiles = in_vmem(three_centre.reshape(TILES, BS * BS, NAUX))
    share, mask, square = pl.pallas_call(
        prepare_kernel,
        out_shape=(
            jax.ShapeDtypeStruct((NZ * NX, NC, 4, HALF), BF16),
            jax.ShapeDtypeStruct((1, NAUX), F32),
            jax.ShapeDtypeStruct((8, 128), F32),
        ),
        in_specs=[VMEM] * 3,
        out_specs=(VMEM, VMEM, VMEM),
        name="prepare",
    )(block_sizes.reshape(1, BLOCKS), adjoint, vir_density)
    share = share.reshape(NZ * NX * NC, 4, HALF)
    own = lax.all_to_all(share, ("z", "x", "c"), 0, 0, tiled=True).reshape(NZ, 32, HALF)
    ahead = [(i, (i + 1) % NY) for i in range(NY)]
    behind = [(i, (i - 1) % NY) for i in range(NY)]

    def sibling(x):
        return lax.ppermute(x, "c", [(0, 1), (1, 0)])

    def shift(x, pairs):
        return lax.ppermute(x, "y", pairs)

    m1 = shift(own, ahead)
    m3 = shift(own, behind)
    s0 = sibling(own)
    oexp, meta, first = expand(tile_rows, col_owner, col_block, block_sizes, occ_density)
    s0, oexp, meta, first = lax.optimization_barrier((s0, oexp, meta, first))
    c0, token = contract(tiles, [own], [s0], own, "contract_own")
    m1, m3, token = lax.optimization_barrier((m1, m3, token))
    m2a = shift(m1[: NZ // 2], ahead)
    m2b = shift(m3[NZ // 2 :], behind)
    s1 = sibling(m1)
    s3 = sibling(m3)
    c1, c3, token = contract(tiles, [m1, m3], [s1, s3], token, "contract_sides")
    m2a, m2b, token = lax.optimization_barrier((m2a, m2b, token))
    s2a = sibling(m2a)
    s2b = sibling(m2b)

    pay = form(
        tiles, oexp, meta, first,
        (own, m1, m3, s0, s1, s3, m2a, m2b, s2a, s2b, c0, c1, c3, token),
    )
    got = lax.all_to_all(pay, ("x", "c"), 0, 0, tiled=True)
    occ_grad, terms = pl.pallas_call(
        route_kernel,
        out_shape=(
            jax.ShapeDtypeStruct((1, NAUX), F32),
            jax.ShapeDtypeStruct((NZ * NY, 8, 128), BF16),
        ),
        in_specs=[VMEM, VMEM],
        out_specs=(VMEM, VMEM),
        scratch_shapes=[pltpu.VMEM((NZ * NY, 8, 128), F32)],
        name="route",
    )(mask, got)
    back = lax.all_to_all(terms, ("z", "y"), 0, 0, tiled=True)
    vir_grad = jnp.sum(back.astype(F32) * square, axis=0).reshape(1, NAUX)
    return occ_grad, vir_grad


def solution(mesh):
    grid = Mesh(mesh.devices.reshape(NZ, NY, NX, NC), ("z", "y", "x", "c"))
    every = ("z", "y", "x", "c")
    blk = ("z", "y")
    in_specs = (
        P(every, None),
        P(every, None, None, None),
        P(blk, None),
        P(blk, None),
        P(blk),
        P(every),
        P(every, None),
        P(every),
    )
    out_specs = (P(every, None), P(every, None))
    return jax.shard_map(shards, mesh=grid, in_specs=in_specs, out_specs=out_specs, check_vma=False)
```

```python
import functools
import jax
import jax.numpy as jnp
from jax import lax
from jax.experimental import pallas as pl
from jax.experimental.pallas import tpu as pltpu
from jax.sharding import Mesh, PartitionSpec as P

BS = 32
NAUX = 1024
HALF = 640
NZ, NY, NX, NC = 8, 4, 4, 2
TILES = 4
BLOCKS = 8
F32 = jnp.float32
BF16 = jnp.bfloat16
NORM = NAUX ** -0.5
PAY = NAUX + 128
ANY = pl.BlockSpec(memory_space=pl.ANY)
SMEM = pl.BlockSpec(memory_space=pltpu.SMEM)
VMEM = pl.BlockSpec(memory_space=pltpu.VMEM)


def dot(a, b, ca, cb):
    return lax.dot_general(a, b, (((ca,), (cb,)), ((), ())), preferred_element_type=F32)


def iota(shape, dim):
    return lax.broadcasted_iota(jnp.int32, shape, dim)


def pair_mask(size):
    return live_mask(iota((1, NAUX), 1), size)


def live_mask(pair, size):
    return ((pair // BS < size) & (pair % BS < size)).astype(F32)


def pick_row(block, row):
    return jnp.sum(jnp.where(iota(block.shape, 0) == row, block.astype(F32), 0.0), axis=0, keepdims=True)


def prepare_kernel(sizes_ref, adj_ref, vir_ref, out_ref, mask_ref, square_ref):
    aux = lax.axis_index("x") * NC + lax.axis_index("c")
    size = jnp.sum(jnp.where(iota((1, BLOCKS), 1) == aux, sizes_ref[...], 0), axis=1, keepdims=True)
    mask = pair_mask(size)
    mask_ref[...] = mask * NORM
    square_ref[...] = live_mask(iota((8, 128), 0) * 128 + iota((8, 128), 1), size) * NORM
    row = (pick_row(vir_ref[...], aux) * mask).astype(BF16)
    quarters = jnp.concatenate([row[:, 256 * r : 256 * (r + 1)] for r in range(4)], axis=0)
    for c in range(NC):
        share = jnp.concatenate(
            [adj_ref[:, 512 * c : 512 * (c + 1)], quarters[:, 128 * c : 128 * (c + 1)]], axis=1
        )
        out_ref[:, c] = jnp.broadcast_to(share[None], (NZ * NX, 4, HALF))


def row_sums(parts):
    row = iota(parts[0].shape, 0)
    for step in (1, 2, 4):
        first = row // step % 2 == 0
        parts = [
            jnp.where(first, a, b) + pltpu.roll(jnp.where(first, b, a), step, 0)
            for a, b in zip(parts[::2], parts[1::2])
        ]
    return parts[0]


def chunk_slots(y):
    return [lax.rem(y + NY - shift, NY) for shift in (0, 1, 3, 2)]


def half_lanes(half, width):
    return pl.ds(pl.multiple_of(half * width, width), width)


def contract_kernel(count, tile_ref, *refs):
    mine, other = refs[:count], refs[count : 2 * count]
    outs = refs[2 * count + 1 : 3 * count + 1]
    token, adj, sem = refs[3 * count + 1 :]
    c = lax.axis_index("c")

    def copies():
        found = []
        for half, group in ((c, mine), (1 - c, other)):
            for m, src in enumerate(group):
                found.append(pltpu.make_async_copy(
                    src.at[:, :, pl.ds(0, 512)], adj.at[m, :, :, half_lanes(half, 512)], sem.at[len(found)]))
        return found

    @pl.when(pl.program_id(0) == 0)
    def _():
        for copy in copies():
            copy.start()
        token[...] = jnp.zeros_like(token)
        for copy in copies():
            copy.wait()

    t = pl.program_id(0)
    for m in range(count):
        a = adj[m].reshape(256, NAUX)
        for n in range(4):
            lanes = slice(256 * n, 256 * (n + 1))
            outs[m][0, :, :, lanes] = dot(a, tile_ref[t, lanes, :], 1, 1).astype(BF16).reshape(NZ, 32, 256)


def in_hbm(x):
    return pltpu.with_memory_space_constraint(x, pltpu.HBM)


def in_vmem(x):
    return pltpu.with_memory_space_constraint(x, pltpu.VMEM)


def contract(tiles, mine, other, after, name):
    count = len(mine)
    return pl.pallas_call(
        functools.partial(contract_kernel, count),
        grid=(TILES,),
        in_specs=[VMEM] + [ANY] * (2 * count + 1),
        out_specs=[pl.BlockSpec((1, NZ, 32, NAUX), lambda t: (t, 0, 0, 0))] * count
        + [pl.BlockSpec((8, 128), lambda t: (0, 0))],
        out_shape=[jax.ShapeDtypeStruct((TILES, NZ, 32, NAUX), BF16)] * count
        + [jax.ShapeDtypeStruct((8, 128), F32)],
        scratch_shapes=[
            pltpu.VMEM((count, NZ, 32, NAUX), BF16),
            pltpu.SemaphoreType.DMA((2 * count,)),
        ],
        compiler_params=pltpu.CompilerParams(vmem_limit_bytes=20 << 20),
        cost_estimate=pl.CostEstimate(
            flops=2 * count * TILES * NAUX * NAUX * 256, bytes_accessed=(8 + 2 * count) << 20, transcendentals=0
        ),
        name=name,
    )(tiles, *mine, *other, after)


def expand_kernel(rows, owners, blocks, sizes, occ_ref, oexp_ref, meta_ref, first_ref):
    same = (iota((128, 128), 0) // BS == iota((128, 128), 1) // BS).astype(BF16)
    for t in range(TILES):
        r = rows[t]
        occ_row = pick_row(occ_ref[...], r) * pair_mask(sizes[r])
        occ_sel = jnp.where(iota((BS, NAUX), 0) == iota((BS, NAUX), 1) % BS, occ_row, 0.0).astype(BF16)
        for m in range(8):
            lanes = slice(128 * m, 128 * (m + 1))
            oexp_ref[t, :, lanes] = dot(occ_sel[:, lanes], same, 1, 0)
        for n, value in enumerate((r, blocks[t], owners[t])):
            meta_ref[t, n] = jnp.full((8, 128), value, jnp.int32)
        col = owners[t] * BLOCKS + blocks[t]
        first_ref[t * BS : (t + 1) * BS, :] = 4 * col + iota((BS, 128), 0) // 8


def expand(tile_rows, col_owner, col_block, block_sizes, occ_density):
    return pl.pallas_call(
        expand_kernel,
        in_specs=[SMEM] * 4 + [VMEM],
        out_specs=[VMEM] * 3,
        out_shape=[
            jax.ShapeDtypeStruct((TILES, BS, NAUX), F32),
            jax.ShapeDtypeStruct((TILES, 3, 8, 128), jnp.int32),
            jax.ShapeDtypeStruct((TILES * BS, 128), jnp.int32),
        ],
        name="expand",
    )(tile_rows, col_owner.reshape(TILES), col_block, block_sizes, occ_density)


def tile_kernel(
    tile_ref, oexp, meta_ref, first_ref,
    m0, m1, m3, s0, s1, s3, m2a, m2b, s2a, s2b, c0, c1, c3, after, pay_ref,
    adj, vir, ct, g_ref, vexp, vacc, oacc, pay, occ_sum, sem, ct_sem,
):
    t = pl.program_id(0)
    y = lax.axis_index("y")
    c = lax.axis_index("c")
    slots = chunk_slots(y)
    width = 256
    chunks = NAUX // width

    def gathered():
        found = []

        def add(src, dst):
            found.append(pltpu.make_async_copy(src, dst, sem.at[len(found)]))

        for half, group, last in ((c, (m0, m1, m3), (m2a, m2b)), (1 - c, (s0, s1, s3), (s2a, s2b))):
            for src, at in zip(group, slots):
                add(src.at[:, :, pl.ds(512, 128)], vir.at[:, at, :, half_lanes(half, 128)])
            for n, src in enumerate(last):
                part = pl.ds(n * (NZ // 2), NZ // 2)
                add(src.at[:, :, pl.ds(512, 128)], vir.at[part, slots[3], :, half_lanes(half, 128)])
                add(src.at[:, :, pl.ds(0, 512)], adj.at[part, :, half_lanes(half, 512)])
        return found

    def contracted(tile):
        b = lax.rem(tile, 2)
        return [
            pltpu.make_async_copy(src.at[tile], ct.at[b, :, at], ct_sem.at[b, n])
            for n, (src, at) in enumerate(zip((c0, c1, c3), slots))
        ]

    @pl.when(t == 0)
    def _():
        for copy in gathered() + contracted(0):
            copy.start()
        pay[...] = jnp.zeros_like(pay)
        pay[:, :, NAUX:] = jnp.full((BLOCKS, 8, 128), -1.0, F32)
        occ_sum[...] = jnp.zeros_like(occ_sum)
        for copy in gathered():
            copy.wait()
        pick = jnp.concatenate(
            [first_ref[...] == iota((TILES * BS, 128), 1) + 128 * m for m in range(8)], axis=1
        ).astype(BF16)
        spread = dot(pick, vir[...].reshape(NAUX, 256), 1, 0)
        group = iota((TILES * BS, 256), 1) // BS == iota((TILES * BS, 256), 0) % 8
        spread = jnp.where(group, spread, 0.0).astype(BF16)
        fold = (iota((256, BS), 0) % BS == iota((256, BS), 1)).astype(BF16)
        v_blocks = dot(spread, fold, 1, 0).astype(BF16)
        repeat = (iota((BS, NAUX), 0) == iota((BS, NAUX), 1) % BS).astype(BF16)
        for tile in range(TILES):
            vexp[tile] = dot(v_blocks[tile * BS : (tile + 1) * BS], repeat, 0, 0)

    @pl.when(t + 1 < TILES)
    def _():
        for copy in contracted(t + 1):
            copy.start()

    @pl.when(t < TILES)
    def _():
        for copy in contracted(t):
            copy.wait()

    def reduce(n, tile):
        lanes = slice(n * width, (n + 1) * width)
        vx = vexp[tile, :, lanes]
        acc = jnp.zeros((BS, width), F32)
        for base in range(0, BS, 8):
            parts = []
            for l in range(base, base + 8):
                g = g_ref[n % 2, l * BS : (l + 1) * BS, :]
                acc = acc + oexp[tile, l : l + 1, lanes] * g
                p = vx * g
                parts.append((p[:8] + p[8:16]) + (p[16:24] + p[24:]))
            oacc[base : base + 8, lanes] = row_sums(parts)
        vacc[:, lanes] = acc

    def flat(x):
        x = jnp.concatenate([x] * 4, axis=0).T[:BS]
        x = jnp.concatenate([x] * 8, axis=1)
        x = jnp.where(iota((BS, NAUX), 0) == iota((BS, NAUX), 1) // BS, x, 0.0)
        return jnp.sum(x, axis=0, keepdims=True)

    def collect(tile, valid):
        va = vacc[...]
        virt = va[:, :128]
        for m in range(1, 8):
            virt = virt + va[:, m * 128 : (m + 1) * 128]
        virt = virt + pltpu.roll(virt, 64, 1)
        virt = virt + pltpu.roll(virt, 32, 1)
        oa = oacc[...]
        high = oa.astype(BF16)
        rest = oa - high.astype(F32)
        low = rest.astype(BF16)
        group = (iota((NAUX, 128), 0) // BS == iota((NAUX, 128), 1) % BS).astype(BF16)
        occt = dot(high, group, 1, 0) + dot(low, group, 1, 0)
        dest = iota((BLOCKS, 128), 0)
        row_here = jnp.concatenate([dest == meta_ref[tile, 0]] * 8, axis=1)
        block_here = dest == meta_ref[tile, 1]
        occ_sum[...] += jnp.where(row_here & valid, flat(occt), 0.0)
        mine = jnp.where(jnp.concatenate([block_here] * 8, axis=1), flat(virt), 0.0)
        label = jnp.where(block_here, meta_ref[tile, 2].astype(F32), -1.0)
        whole = jnp.concatenate([mine, label], axis=1)
        pay[...] = jnp.where((iota((BLOCKS, 8, PAY), 1) == tile) & valid, whole[:, None, :], pay[...])

    @pl.when(t < TILES)
    def _():
        reduce(chunks - 1, jnp.maximum(t - 1, 0))
        b = lax.rem(t, 2)
        a = adj[...].reshape(256, NAUX)
        for n in range(chunks):
            lanes = slice(n * width, (n + 1) * width)
            ct[b, :, slots[3], :, lanes] = dot(a, tile_ref[t, lanes, :], 1, 1).astype(BF16).reshape(NZ, 32, width)
        def gram(n):
            lanes = slice(n * width, (n + 1) * width)
            g_ref[n % 2] = dot(tile_ref[t], ct[b, :, :, :, lanes].reshape(NAUX, width), 1, 0)

        collect(jnp.maximum(t - 1, 0), t > 0)
        gram(0)
        for n in range(1, chunks):
            gram(n)
            reduce(n - 1, t)

    @pl.when(t == TILES)
    def _():
        reduce(chunks - 1, TILES - 1)
        collect(TILES - 1, True)
        total = occ_sum[...]
        top = total.astype(BF16).astype(F32)
        pay[:, 4:5, :NAUX] = top[:, None, :]
        pay[:, 5:6, :NAUX] = (total - top)[:, None, :]
        pay_ref[...] = pay[...].astype(BF16)


def form(tiles, oexp, meta, first, gathered):
    return pl.pallas_call(
        tile_kernel,
        grid=(TILES + 1,),
        in_specs=[VMEM] * 4 + [ANY] * 14,
        out_specs=pl.BlockSpec((BLOCKS, 8, PAY), lambda t: (0, 0, 0)),
        scratch_shapes=[
            pltpu.VMEM((NZ, 32, NAUX), BF16),
            pltpu.VMEM((NZ, NY, 32, 256), BF16),
            pltpu.VMEM((2, NZ, NY, 32, NAUX), BF16),
            pltpu.VMEM((2, NAUX, 256), F32),
            pltpu.VMEM((TILES, BS, NAUX), F32),
            pltpu.VMEM((BS, NAUX), F32),
            pltpu.VMEM((BS, NAUX), F32),
            pltpu.VMEM((BLOCKS, 8, PAY), F32),
            pltpu.VMEM((BLOCKS, NAUX), F32),
            pltpu.SemaphoreType.DMA((14,)),
            pltpu.SemaphoreType.DMA((2, 3)),
        ],
        out_shape=jax.ShapeDtypeStruct((BLOCKS, 8, PAY), BF16),
        compiler_params=pltpu.CompilerParams(vmem_limit_bytes=24 << 20),
        cost_estimate=pl.CostEstimate(flops=11 << 30, bytes_accessed=16 << 20, transcendentals=0),
        name="tiles",
    )(tiles, oexp, meta, first, *gathered)


def route_kernel(mask_ref, got_ref, occ_ref, out_ref, spread):
    got = got_ref[...].astype(F32)
    occ = jnp.sum(got[:, 4, :NAUX] + got[:, 5, :NAUX], axis=0, keepdims=True)
    occ_ref[...] = occ * mask_ref[...]
    flat = got.reshape(8 * BLOCKS, PAY)
    hot = (flat[:, NAUX:] == iota((8 * BLOCKS, 128), 1).astype(F32)).astype(BF16)
    terms = dot(hot, flat[:, :NAUX].astype(BF16), 0, 0)[: NZ * NY]
    for s in range(8):
        spread[:, s, :] = terms[:, 128 * s : 128 * (s + 1)]
    out_ref[...] = spread[...].astype(BF16)


def shards(adjoint, three_centre, occ_density, vir_density, block_sizes, tile_rows, col_owner, col_block):
    tiles = in_vmem(three_centre.reshape(TILES, BS * BS, NAUX))
    share, mask, square = pl.pallas_call(
        prepare_kernel,
        out_shape=(
            pltpu.VMEM((NZ * NX, NC, 4, HALF), BF16),
            pltpu.VMEM((1, NAUX), F32),
            pltpu.VMEM((8, 128), F32),
        ),
        in_specs=[VMEM] * 3,
        out_specs=(VMEM, VMEM, VMEM),
        name="prepare",
    )(block_sizes.reshape(1, BLOCKS), adjoint, vir_density)
    share = share.reshape(NZ * NX * NC, 4, HALF)
    own = lax.all_to_all(share, ("z", "x", "c"), 0, 0, tiled=True).reshape(NZ, 32, HALF)
    ahead = [(i, (i + 1) % NY) for i in range(NY)]
    behind = [(i, (i - 1) % NY) for i in range(NY)]

    def sibling(x):
        return lax.ppermute(x, "c", [(0, 1), (1, 0)])

    def shift(x, pairs):
        return lax.ppermute(x, "y", pairs)

    m1 = shift(own, ahead)
    m3 = shift(own, behind)
    s0 = sibling(own)
    oexp, meta, first = expand(tile_rows, col_owner, col_block, block_sizes, occ_density)
    s0, oexp, meta, first = lax.optimization_barrier((s0, oexp, meta, first))
    c0, token = contract(tiles, [own], [s0], own, "contract_own")
    m1, m3, token = lax.optimization_barrier((m1, m3, token))
    m2a = shift(m1[: NZ // 2], ahead)
    m2b = shift(m3[NZ // 2 :], behind)
    s1 = sibling(m1)
    s3 = sibling(m3)
    c1, c3, token = contract(tiles, [m1, m3], [s1, s3], token, "contract_sides")
    m2a, m2b, token = lax.optimization_barrier((m2a, m2b, token))
    s2a = sibling(m2a)
    s2b = sibling(m2b)

    pay = form(
        tiles, oexp, meta, first,
        (own, m1, m3, s0, s1, s3, m2a, m2b, s2a, s2b, c0, c1, c3, token),
    )
    got = lax.all_to_all(pay, ("x", "c"), 0, 0, tiled=True)
    occ_grad, terms = pl.pallas_call(
        route_kernel,
        out_shape=(
            jax.ShapeDtypeStruct((1, NAUX), F32),
            pltpu.VMEM((NZ * NY, 8, 128), BF16),
        ),
        in_specs=[VMEM, VMEM],
        out_specs=(VMEM, VMEM),
        scratch_shapes=[pltpu.VMEM((NZ * NY, 8, 128), F32)],
        name="route",
    )(in_vmem(mask), in_vmem(got))
    back = lax.all_to_all(terms, ("z", "y"), 0, 0, tiled=True)
    vir_grad = jnp.sum(back.astype(F32) * square, axis=0).reshape(1, NAUX)
    return occ_grad, vir_grad


def solution(mesh):
    grid = Mesh(mesh.devices.reshape(NZ, NY, NX, NC), ("z", "y", "x", "c"))
    every = ("z", "y", "x", "c")
    blk = ("z", "y")
    in_specs = (
        P(every, None),
        P(every, None, None, None),
        P(blk, None),
        P(blk, None),
        P(blk),
        P(every),
        P(every, None),
        P(every),
    )
    out_specs = (P(every, None), P(every, None))
    return jax.shard_map(shards, mesh=grid, in_specs=in_specs, out_specs=out_specs, check_vma=False)
```

```python
import functools
import jax
import jax.numpy as jnp
from jax import lax
from jax.experimental import pallas as pl
from jax.experimental.pallas import tpu as pltpu
from jax.sharding import Mesh, PartitionSpec as P

BS = 32
NAUX = 1024
HALF = 640
NZ, NY, NX, NC = 8, 4, 4, 2
TILES = 4
BLOCKS = 8
F32 = jnp.float32
BF16 = jnp.bfloat16
NORM = NAUX ** -0.5
SLOT = NAUX + 128
PAY = SLOT + 512
ANY = pl.BlockSpec(memory_space=pl.ANY)
SMEM = pl.BlockSpec(memory_space=pltpu.SMEM)
VMEM = pl.BlockSpec(memory_space=pltpu.VMEM)


def dot(a, b, ca, cb):
    return lax.dot_general(a, b, (((ca,), (cb,)), ((), ())), preferred_element_type=F32)


def iota(shape, dim):
    return lax.broadcasted_iota(jnp.int32, shape, dim)


def pair_mask(size):
    return live_mask(iota((1, NAUX), 1), size)


def live_mask(pair, size):
    return ((pair // BS < size) & (pair % BS < size)).astype(F32)


def pick_row(block, row):
    return jnp.sum(jnp.where(iota(block.shape, 0) == row, block.astype(F32), 0.0), axis=0, keepdims=True)


def prepare_kernel(sizes_ref, adj_ref, vir_ref, out_ref, mask_ref, square_ref):
    aux = lax.axis_index("x") * NC + lax.axis_index("c")
    size = jnp.sum(jnp.where(iota((1, BLOCKS), 1) == aux, sizes_ref[...], 0), axis=1, keepdims=True)
    mask = pair_mask(size)
    mask_ref[...] = mask * NORM
    square_ref[...] = live_mask(iota((8, 128), 0) * 128 + iota((8, 128), 1), size) * NORM
    row = (pick_row(vir_ref[...], aux) * mask).astype(BF16)
    quarters = jnp.concatenate([row[:, 256 * r : 256 * (r + 1)] for r in range(4)], axis=0)
    for c in range(NC):
        share = jnp.concatenate(
            [adj_ref[:, 512 * c : 512 * (c + 1)], quarters[:, 128 * c : 128 * (c + 1)]], axis=1
        )
        out_ref[:, c] = jnp.broadcast_to(share[None], (NZ * NX, 4, HALF))


def row_sums(parts):
    row = iota(parts[0].shape, 0)
    for step in (1, 2, 4):
        first = row // step % 2 == 0
        parts = [
            jnp.where(first, a, b) + pltpu.roll(jnp.where(first, b, a), step, 0)
            for a, b in zip(parts[::2], parts[1::2])
        ]
    return parts[0]


def chunk_slots(y):
    return [lax.rem(y + NY - shift, NY) for shift in (0, 1, 3, 2)]


def half_lanes(half, width):
    return pl.ds(pl.multiple_of(half * width, width), width)


def contract_kernel(count, tile_ref, *refs):
    mine, other = refs[:count], refs[count : 2 * count]
    outs = refs[2 * count + 1 : 3 * count + 1]
    token, adj, sem = refs[3 * count + 1 :]
    c = lax.axis_index("c")

    def copies():
        found = []
        for half, group in ((c, mine), (1 - c, other)):
            for m, src in enumerate(group):
                found.append(pltpu.make_async_copy(
                    src.at[:, :, pl.ds(0, 512)], adj.at[m, :, :, half_lanes(half, 512)], sem.at[len(found)]))
        return found

    @pl.when(pl.program_id(0) == 0)
    def _():
        for copy in copies():
            copy.start()
        token[...] = jnp.zeros_like(token)
        for copy in copies():
            copy.wait()

    t = pl.program_id(0)
    for m in range(count):
        a = adj[m].reshape(256, NAUX)
        for n in range(4):
            lanes = slice(256 * n, 256 * (n + 1))
            outs[m][0, :, :, lanes] = dot(a, tile_ref[t, lanes, :], 1, 1).astype(BF16).reshape(NZ, 32, 256)


def in_hbm(x):
    return pltpu.with_memory_space_constraint(x, pltpu.HBM)


def in_vmem(x):
    return pltpu.with_memory_space_constraint(x, pltpu.VMEM)


def contract(tiles, mine, other, after, name):
    count = len(mine)
    return pl.pallas_call(
        functools.partial(contract_kernel, count),
        grid=(TILES,),
        in_specs=[VMEM] + [ANY] * (2 * count + 1),
        out_specs=[pl.BlockSpec((1, NZ, 32, NAUX), lambda t: (t, 0, 0, 0))] * count
        + [pl.BlockSpec((8, 128), lambda t: (0, 0))],
        out_shape=[jax.ShapeDtypeStruct((TILES, NZ, 32, NAUX), BF16)] * count
        + [jax.ShapeDtypeStruct((8, 128), F32)],
        scratch_shapes=[
            pltpu.VMEM((count, NZ, 32, NAUX), BF16),
            pltpu.SemaphoreType.DMA((2 * count,)),
        ],
        compiler_params=pltpu.CompilerParams(vmem_limit_bytes=20 << 20),
        cost_estimate=pl.CostEstimate(
            flops=2 * count * TILES * NAUX * NAUX * 256, bytes_accessed=(8 + 2 * count) << 20, transcendentals=0
        ),
        name=name,
    )(tiles, *mine, *other, after)


def expand_kernel(rows, owners, blocks, sizes, occ_ref, oexp_ref, meta_ref, first_ref):
    same = (iota((128, 128), 0) // BS == iota((128, 128), 1) // BS).astype(BF16)
    for t in range(TILES):
        r = rows[t]
        occ_row = pick_row(occ_ref[...], r) * pair_mask(sizes[r])
        occ_sel = jnp.where(iota((BS, NAUX), 0) == iota((BS, NAUX), 1) % BS, occ_row, 0.0).astype(BF16)
        for m in range(8):
            lanes = slice(128 * m, 128 * (m + 1))
            oexp_ref[t, :, lanes] = dot(occ_sel[:, lanes], same, 1, 0)
        for n, value in enumerate((r, blocks[t], owners[t])):
            meta_ref[t, n] = jnp.full((8, 128), value, jnp.int32)
        col = owners[t] * BLOCKS + blocks[t]
        first_ref[t * BS : (t + 1) * BS, :] = 4 * col + iota((BS, 128), 0) // 8


def expand(tile_rows, col_owner, col_block, block_sizes, occ_density):
    return pl.pallas_call(
        expand_kernel,
        in_specs=[SMEM] * 4 + [VMEM],
        out_specs=[VMEM] * 3,
        out_shape=[
            jax.ShapeDtypeStruct((TILES, BS, NAUX), F32),
            jax.ShapeDtypeStruct((TILES, 3, 8, 128), jnp.int32),
            jax.ShapeDtypeStruct((TILES * BS, 128), jnp.int32),
        ],
        name="expand",
    )(tile_rows, col_owner.reshape(TILES), col_block, block_sizes, occ_density)


def tile_kernel(
    tile_ref, oexp, meta_ref, first_ref,
    m0, m1, m3, s0, s1, s3, m2a, m2b, s2a, s2b, c0, c1, c3, after, pay_ref,
    adj, vir, ct, g_ref, vexp, vacc, oacc, pay, occ_sum, sem, ct_sem,
):
    t = pl.program_id(0)
    y = lax.axis_index("y")
    c = lax.axis_index("c")
    slots = chunk_slots(y)
    width = 256
    chunks = NAUX // width

    def gathered():
        found = []

        def add(src, dst):
            found.append(pltpu.make_async_copy(src, dst, sem.at[len(found)]))

        for half, group, last in ((c, (m0, m1, m3), (m2a, m2b)), (1 - c, (s0, s1, s3), (s2a, s2b))):
            for src, at in zip(group, slots):
                add(src.at[:, :, pl.ds(512, 128)], vir.at[:, at, :, half_lanes(half, 128)])
            for n, src in enumerate(last):
                part = pl.ds(n * (NZ // 2), NZ // 2)
                add(src.at[:, :, pl.ds(512, 128)], vir.at[part, slots[3], :, half_lanes(half, 128)])
                add(src.at[:, :, pl.ds(0, 512)], adj.at[part, :, half_lanes(half, 512)])
        return found

    def contracted(tile):
        b = lax.rem(tile, 2)
        return [
            pltpu.make_async_copy(src.at[tile], ct.at[b, :, at], ct_sem.at[b, n])
            for n, (src, at) in enumerate(zip((c0, c1, c3), slots))
        ]

    @pl.when(t == 0)
    def _():
        for copy in gathered() + contracted(0):
            copy.start()
        pay[...] = jnp.zeros_like(pay)
        pay[:, :, NAUX:SLOT] = jnp.full((BLOCKS, TILES, 128), -1.0, F32)
        occ_sum[...] = jnp.zeros_like(occ_sum)
        for copy in gathered():
            copy.wait()
        pick = jnp.concatenate(
            [first_ref[...] == iota((TILES * BS, 128), 1) + 128 * m for m in range(8)], axis=1
        ).astype(BF16)
        spread = dot(pick, vir[...].reshape(NAUX, 256), 1, 0)
        group = iota((TILES * BS, 256), 1) // BS == iota((TILES * BS, 256), 0) % 8
        spread = jnp.where(group, spread, 0.0).astype(BF16)
        fold = (iota((256, BS), 0) % BS == iota((256, BS), 1)).astype(BF16)
        v_blocks = dot(spread, fold, 1, 0).astype(BF16)
        repeat = (iota((BS, NAUX), 0) == iota((BS, NAUX), 1) % BS).astype(BF16)
        for tile in range(TILES):
            vexp[tile] = dot(v_blocks[tile * BS : (tile + 1) * BS], repeat, 0, 0)

    @pl.when(t + 1 < TILES)
    def _():
        for copy in contracted(t + 1):
            copy.start()

    @pl.when(t < TILES)
    def _():
        for copy in contracted(t):
            copy.wait()

    def reduce(n, tile):
        lanes = slice(n * width, (n + 1) * width)
        vx = vexp[tile, :, lanes]
        acc = jnp.zeros((BS, width), F32)
        for base in range(0, BS, 8):
            parts = []
            for l in range(base, base + 8):
                g = g_ref[n % 2, l * BS : (l + 1) * BS, :]
                acc = acc + oexp[tile, l : l + 1, lanes] * g
                p = vx * g
                parts.append((p[:8] + p[8:16]) + (p[16:24] + p[24:]))
            oacc[base : base + 8, lanes] = row_sums(parts)
        vacc[:, lanes] = acc

    def flat(x):
        x = jnp.concatenate([x] * 4, axis=0).T[:BS]
        x = jnp.concatenate([x] * 8, axis=1)
        x = jnp.where(iota((BS, NAUX), 0) == iota((BS, NAUX), 1) // BS, x, 0.0)
        return jnp.sum(x, axis=0, keepdims=True)

    def collect(tile, valid):
        va = vacc[...]
        virt = va[:, :128]
        for m in range(1, 8):
            virt = virt + va[:, m * 128 : (m + 1) * 128]
        virt = virt + pltpu.roll(virt, 64, 1)
        virt = virt + pltpu.roll(virt, 32, 1)
        oa = oacc[...]
        high = oa.astype(BF16)
        rest = oa - high.astype(F32)
        low = rest.astype(BF16)
        group = (iota((NAUX, 128), 0) // BS == iota((NAUX, 128), 1) % BS).astype(BF16)
        occt = dot(high, group, 1, 0) + dot(low, group, 1, 0)
        dest = iota((BLOCKS, 128), 0)
        row_here = jnp.concatenate([dest == meta_ref[tile, 0]] * 8, axis=1)
        block_here = dest == meta_ref[tile, 1]
        occ_sum[...] += jnp.where(row_here & valid, flat(occt), 0.0)
        mine = jnp.where(jnp.concatenate([block_here] * 8, axis=1), flat(virt), 0.0)
        label = jnp.where(block_here, meta_ref[tile, 2].astype(F32), -1.0)
        whole = jnp.concatenate([mine, label], axis=1)
        here = (iota((BLOCKS, TILES, SLOT), 1) == tile) & valid
        pay[:, :, :SLOT] = jnp.where(here, whole[:, None, :], pay[:, :, :SLOT])

    @pl.when(t < TILES)
    def _():
        reduce(chunks - 1, jnp.maximum(t - 1, 0))
        b = lax.rem(t, 2)
        a = adj[...].reshape(256, NAUX)
        for n in range(chunks):
            lanes = slice(n * width, (n + 1) * width)
            ct[b, :, slots[3], :, lanes] = dot(a, tile_ref[t, lanes, :], 1, 1).astype(BF16).reshape(NZ, 32, width)
        def gram(n):
            lanes = slice(n * width, (n + 1) * width)
            g_ref[n % 2] = dot(tile_ref[t], ct[b, :, :, :, lanes].reshape(NAUX, width), 1, 0)

        collect(jnp.maximum(t - 1, 0), t > 0)
        gram(0)
        for n in range(1, chunks):
            gram(n)
            reduce(n - 1, t)

    @pl.when(t == TILES)
    def _():
        reduce(chunks - 1, TILES - 1)
        collect(TILES - 1, True)
        total = occ_sum[...]
        top = total.astype(BF16).astype(F32)
        for n, part in enumerate((top, total - top)):
            for half in range(2):
                row = 2 * n + half
                pay[:, row : row + 1, SLOT:] = part[:, None, 512 * half : 512 * (half + 1)]
        pay_ref[...] = pay[...].astype(BF16)


def form(tiles, oexp, meta, first, gathered):
    return pl.pallas_call(
        tile_kernel,
        grid=(TILES + 1,),
        in_specs=[VMEM] * 4 + [ANY] * 14,
        out_specs=pl.BlockSpec((BLOCKS, TILES, PAY), lambda t: (0, 0, 0)),
        scratch_shapes=[
            pltpu.VMEM((NZ, 32, NAUX), BF16),
            pltpu.VMEM((NZ, NY, 32, 256), BF16),
            pltpu.VMEM((2, NZ, NY, 32, NAUX), BF16),
            pltpu.VMEM((2, NAUX, 256), F32),
            pltpu.VMEM((TILES, BS, NAUX), F32),
            pltpu.VMEM((BS, NAUX), F32),
            pltpu.VMEM((BS, NAUX), F32),
            pltpu.VMEM((BLOCKS, TILES, PAY), F32),
            pltpu.VMEM((BLOCKS, NAUX), F32),
            pltpu.SemaphoreType.DMA((14,)),
            pltpu.SemaphoreType.DMA((2, 3)),
        ],
        out_shape=jax.ShapeDtypeStruct((BLOCKS, TILES, PAY), BF16),
        compiler_params=pltpu.CompilerParams(vmem_limit_bytes=24 << 20),
        cost_estimate=pl.CostEstimate(flops=11 << 30, bytes_accessed=16 << 20, transcendentals=0),
        name="tiles",
    )(tiles, oexp, meta, first, *gathered)


def route_kernel(mask_ref, got_ref, occ_ref, out_ref, spread):
    got = got_ref[...].astype(F32)
    halves = [got[:, half, SLOT:] + got[:, half + 2, SLOT:] for half in range(2)]
    occ = jnp.sum(jnp.concatenate(halves, axis=1), axis=0, keepdims=True)
    occ_ref[...] = occ * mask_ref[...]
    flat = jnp.concatenate([got[:, n, :SLOT] for n in range(TILES)], axis=0)
    hot = (flat[:, NAUX:] == iota((TILES * BLOCKS, 128), 1).astype(F32)).astype(BF16)
    terms = dot(hot, flat[:, :NAUX].astype(BF16), 0, 0)[: NZ * NY]
    for s in range(8):
        spread[:, s, :] = terms[:, 128 * s : 128 * (s + 1)]
    out_ref[...] = spread[...].astype(BF16)


def shards(adjoint, three_centre, occ_density, vir_density, block_sizes, tile_rows, col_owner, col_block):
    tiles = in_vmem(three_centre.reshape(TILES, BS * BS, NAUX))
    share, mask, square = pl.pallas_call(
        prepare_kernel,
        out_shape=(
            pltpu.VMEM((NZ * NX, NC, 4, HALF), BF16),
            pltpu.VMEM((1, NAUX), F32),
            pltpu.VMEM((8, 128), F32),
        ),
        in_specs=[VMEM] * 3,
        out_specs=(VMEM, VMEM, VMEM),
        name="prepare",
    )(block_sizes.reshape(1, BLOCKS), adjoint, vir_density)
    share = share.reshape(NZ * NX * NC, 4, HALF)
    own = lax.all_to_all(share, ("z", "x", "c"), 0, 0, tiled=True).reshape(NZ, 32, HALF)
    ahead = [(i, (i + 1) % NY) for i in range(NY)]
    behind = [(i, (i - 1) % NY) for i in range(NY)]

    def sibling(x):
        return lax.ppermute(x, "c", [(0, 1), (1, 0)])

    def shift(x, pairs):
        return lax.ppermute(x, "y", pairs)

    m1 = shift(own, ahead)
    m3 = shift(own, behind)
    s0 = sibling(own)
    oexp, meta, first = expand(tile_rows, col_owner, col_block, block_sizes, occ_density)
    s0, oexp, meta, first = lax.optimization_barrier((s0, oexp, meta, first))
    c0, token = contract(tiles, [own], [s0], own, "contract_own")
    m1, m3, token = lax.optimization_barrier((m1, m3, token))
    m2a = shift(m1[: NZ // 2], ahead)
    m2b = shift(m3[NZ // 2 :], behind)
    s1 = sibling(m1)
    s3 = sibling(m3)
    c1, c3, token = contract(tiles, [m1, m3], [s1, s3], token, "contract_sides")
    m2a, m2b, token = lax.optimization_barrier((m2a, m2b, token))
    s2a = sibling(m2a)
    s2b = sibling(m2b)

    pay = form(
        tiles, oexp, meta, first,
        (own, m1, m3, s0, s1, s3, m2a, m2b, s2a, s2b, c0, c1, c3, token),
    )
    got = lax.all_to_all(pay, ("x", "c"), 0, 0, tiled=True)
    occ_grad, terms = pl.pallas_call(
        route_kernel,
        out_shape=(
            jax.ShapeDtypeStruct((1, NAUX), F32),
            pltpu.VMEM((NZ * NY, 8, 128), BF16),
        ),
        in_specs=[VMEM, VMEM],
        out_specs=(VMEM, VMEM),
        scratch_shapes=[pltpu.VMEM((NZ * NY, 8, 128), F32)],
        name="route",
    )(in_vmem(mask), in_vmem(got))
    back = lax.all_to_all(terms, ("z", "y"), 0, 0, tiled=True)
    vir_grad = jnp.sum(back.astype(F32) * square, axis=0).reshape(1, NAUX)
    return occ_grad, vir_grad


def solution(mesh):
    grid = Mesh(mesh.devices.reshape(NZ, NY, NX, NC), ("z", "y", "x", "c"))
    every = ("z", "y", "x", "c")
    blk = ("z", "y")
    in_specs = (
        P(every, None),
        P(every, None, None, None),
        P(blk, None),
        P(blk, None),
        P(blk),
        P(every),
        P(every, None),
        P(every),
    )
    out_specs = (P(every, None), P(every, None))
    return jax.shard_map(shards, mesh=grid, in_specs=in_specs, out_specs=out_specs, check_vma=False)
```
